512 devices in a mesh: blk: 64 (over z_hi, y, x, core), grp: 8 (over z_lo).
Axes of the slice: x: 4, y: 4, z: 16 (z_hi: 2, z_lo: 8; z = z_hi * 8 + z_lo), core: 2. Of those that a mesh axis runs over, the one named last changes fastest.
Arguments:
- samples: float32 [32, 16384], P(None, ('blk', 'grp')), may hold values from 0 to 256
- bounds: int32 [2, 32, 8192], P(None, None, 'blk'), may hold values from 0 to 256, as said below
- spread: float32 [32], replicated, may hold values from 2 to 8
- counts: int32 [8192], P('blk'), may hold values from 0 to 2047
Outputs:
- log_estimate: float32 [8192], P('blk')
- spread_grad: float32 [32], replicated
The draws below stay inside these ranges and needn't reach their ends.
Inputs may be any that keep to these rules, and one draw needn't show every extreme that they name: For every query and dimension bounds[0] < bounds[1]; each query restricts exactly 3 dimensions to a width of 16 to 48 cells and has bounds 0 and 256 in all others.
All inputs are finite; a program needn't handle non-finite values.
Results may differ from the reference program's by a relative error of at most 0.0003.
Values sent between devices are 32-bit elements; how exact they have to be, the bound alone decides.
A program may use at most 64 MiB of HBM per device.

```python
import math
import jax
import jax.numpy as jnp
from jax import lax

DIM = 32
GRID = 256
TABLE_ROWS = 1048576
QUERIES = 8192
SAMPLES = 16384


def draw_bounds(key, part):
    key_rank, key_width, key_start = jax.random.split(key, 3)
    scores = jax.random.randint(key_rank, (QUERIES, DIM), 0, 1 << 20) * DIM + jnp.arange(DIM, dtype=jnp.int32)[None, :]
    chosen = lax.top_k(scores, 3)[1]
    picked = jnp.any(chosen[:, :, None] == jnp.arange(DIM, dtype=jnp.int32)[None, None, :], axis=1)
    widths = jax.random.randint(key_width, (QUERIES, DIM), 16, 49)
    starts = jax.random.randint(key_start, (QUERIES, DIM), 0, GRID - widths + 1)
    lower_bound = jnp.where(picked, starts, 0)
    upper_bound = jnp.where(picked, starts + widths, GRID)
    return jnp.stack([lower_bound.T, upper_bound.T]).astype(jnp.int32)


def place_ends(values, own_key, low, high):
    place = [jax.random.randint(jax.random.fold_in(own_key, axis), (), 0, length) for axis, length in enumerate(values.shape)]
    main_axis = values.shape.index(max(values.shape))
    beside = place[:main_axis] + [(place[main_axis] + 1) % values.shape[main_axis]] + place[main_axis + 1:]
    return values.at[tuple(place)].set(low).at[tuple(beside)].set(high)


def block_levels(stream_key, extent, cuts, smallest, largest):
    level = 1.0
    for axis_at, parts in cuts:
        draws = jax.random.uniform(jax.random.fold_in(jax.random.fold_in(stream_key, 6), axis_at), (parts,), jnp.float32, smallest / len(cuts), largest / len(cuts))
        level = level * jnp.repeat(jnp.exp(draws), extent[axis_at] // parts).reshape((-1,) + (1,) * (len(extent) - 1 - axis_at))
    return level


def setup_inputs(seed: int = 0) -> dict:
    key_list = jax.random.split(jax.random.key(seed), 5)
    return {
        "samples": jnp.clip(256.0 * jax.random.uniform(key_list[0], (DIM, SAMPLES), jnp.float32) ** block_levels(key_list[0], (DIM, SAMPLES), ((1, 512),), -0.2, 0.2), 0.0, 256.0),
        "bounds": draw_bounds(jax.random.fold_in(key_list[4], 71), 0),
        "spread": jnp.clip(jnp.exp(jax.random.uniform(key_list[2], (DIM,), jnp.float32, math.log(2.0), math.log(8.0))), 2.0, 8.0),
        "counts": place_ends(jax.random.randint(key_list[3], (QUERIES,), 0, 2048), jax.random.fold_in(key_list[3], 1), 0, 2047).astype(jnp.int32),
    }


root_half = 0.7071067811865476
density_norm = 0.3989422804014327


def box_terms(lower_edge, upper_edge, points, inverse):
    upper_arg = (upper_edge - points) * inverse
    lower_arg = (lower_edge - points) * inverse
    in_box = 0.5 * (lax.erf(upper_arg * root_half) - lax.erf(lower_arg * root_half))
    slopes = density_norm * (lower_arg * jnp.exp(-0.5 * lower_arg * lower_arg) - upper_arg * jnp.exp(-0.5 * upper_arg * upper_arg))
    prefix_prod = jnp.cumprod(in_box, axis=0)
    behind = jnp.flip(jnp.cumprod(jnp.flip(in_box, 0), axis=0), 0)
    unit_row = jnp.ones_like(in_box[:1])
    before = jnp.concatenate([unit_row, prefix_prod[:-1]], 0)
    after_dims = jnp.concatenate([behind[1:], unit_row], 0)
    return prefix_prod[-1], before * after_dims * slopes


def finish(est_sum, counts_float, sample_total, query_total):
    smoothing = 1.0 / TABLE_ROWS
    estimate = est_sum / sample_total
    log_est = jnp.log(estimate + smoothing)
    target = jnp.log(counts_float / TABLE_ROWS + smoothing)
    weight = 2.0 * (log_est - target) / (query_total * (estimate + smoothing))
    return log_est, weight


def reference(samples, bounds, spread, counts):
    lower_edge = bounds[0].astype(jnp.float32)
    upper_edge = bounds[1].astype(jnp.float32)
    inverse = 1.0 / spread
    width_rows = math.gcd(SAMPLES, 64)
    blocks = samples.reshape(DIM, SAMPLES // width_rows, width_rows).transpose(1, 0, 2)

    def advance(running, points):
        totals, gradients = box_terms(lower_edge[:, None, :], upper_edge[:, None, :], points[:, :, None], inverse[:, None, None])
        return (running[0] + totals.sum(axis=0), running[1] + gradients.sum(axis=1)), None

    initial = (jnp.zeros((QUERIES,), jnp.float32), jnp.zeros((DIM, QUERIES), jnp.float32))
    est_sum, grad_sum = lax.scan(advance, initial, blocks)[0]
    log_est, weight = finish(est_sum, counts.astype(jnp.float32), SAMPLES, QUERIES)
    gradient = jnp.dot(grad_sum, weight, precision=lax.Precision.HIGHEST) / SAMPLES
    return log_est, gradient
```

```python
import functools
import math

import jax
import jax.numpy as jnp
from jax import lax
from jax.experimental import pallas as pl
from jax.experimental.pallas import tpu as pltpu
from jax.sharding import PartitionSpec as P

TABLE_ROWS = 1048576
MESH = pl.DeviceIdType.MESH
F32 = jnp.float32
BF16 = jnp.bfloat16

UNIT = math.sqrt(math.log2(math.e) / 2.0)
LOG2E = math.log2(math.e)
ERF_COEFS = (
    0.939437726891315,
    0.059304200409920856,
    -7.37546114627212e-05,
    -0.00017348738576916883,
    1.7241095109019066e-05,
    -7.97342195757559e-07,
    1.4676678471795133e-08,
)
SLOPE_SCALE = 2.0 / (math.sqrt(2.0 * math.pi) * UNIT)

GRID = 256
ROWS_PER_HALF = 7 * 128
DEPTH = 208


def erf_and_moment(v):
    w = v * v
    poly = jnp.full_like(w, ERF_COEFS[-1])
    for coef in ERF_COEFS[-2::-1]:
        poly = poly * w + coef
    return jnp.tanh(v * poly), v * jnp.exp2(-w)


def split3(x):
    high = x.astype(BF16)
    rest = x - high.astype(F32)
    middle = rest.astype(BF16)
    low = (rest - middle.astype(F32)).astype(BF16)
    return high, middle, low


def dot(a, b, a_dim, b_dim):
    return lax.dot_general(
        a, b, (((a_dim,), (b_dim,)), ((), ())), preferred_element_type=F32
    )


def row_sums(x):
    ones = jnp.ones((8, x.shape[1]), BF16)
    total = None
    for piece in split3(x):
        term = dot(ones, piece, 1, 1)
        total = term if total is None else total + term
    return total[:1]


def kernel(
    sizes,
    sample_total,
    query_total,
    samples_ref,
    bounds_ref,
    spread_ref,
    counts_ref,
    log_ref,
    grad_ref,
    table,
    pieces,
    chosen,
    args,
    inside,
    slopes,
    sums,
    est,
    grad_z,
    grad_a,
    grad_y,
    table_sems,
    a_sems,
    y_sems,
    est_sems,
    gz_sems,
    ga_sems,
    gy_sems,
):
    n_hi, n_y, n_a, n_lo = sizes
    n_z = n_hi * n_lo
    dims = samples_ref.shape[0]
    width = samples_ref.shape[1] * n_a
    blk = lax.axis_index("blk")
    z_lo = lax.axis_index("grp")
    z_hi = blk // (n_y * n_a)
    y = (blk // n_a) % n_y
    a = blk % n_a
    z = z_hi * n_lo + z_lo

    def at_z(step):
        other = (z + step) % n_z
        return ((other // n_lo) * (n_y * n_a) + y * n_a + a, other % n_lo)

    def at_a(step):
        return (z_hi * (n_y * n_a) + y * n_a + (a + step) % n_a, z_lo)

    def at_y(step):
        return (z_hi * (n_y * n_a) + ((y + step) % n_y) * n_a + a, z_lo)

    partner = ((1 - z_hi) * (n_y * n_a) + y * n_a + a, z_lo)

    barrier = pltpu.get_barrier_semaphore()
    peers = [at_z(i) for i in range(1, n_z)]
    peers += [at_a(i) for i in range(1, n_a)]
    peers += [at_y(i) for i in range(1, n_y)]
    for peer in peers:
        pl.semaphore_signal(barrier, inc=1, device_id=peer, device_id_type=MESH)

    def send(src, dst, sems, slot, peer):
        copy = pltpu.make_async_remote_copy(
            src_ref=src,
            dst_ref=dst,
            send_sem=sems.at[0, slot],
            recv_sem=sems.at[1, slot],
            device_id=peer,
            device_id_type=MESH,
        )
        copy.start()
        return copy

    x = samples_ref[...]
    pieces[y, a] = jnp.concatenate(
        [x[8 * i : 8 * i + 8] for i in range(dims // 8)], axis=1
    )
    inverse = UNIT / spread_ref[...]
    eye = lax.broadcasted_iota(jnp.int32, (dims, dims), 0) == lax.broadcasted_iota(
        jnp.int32, (dims, dims), 1
    )
    inverse = jnp.sum(jnp.where(eye, inverse, 0.0), axis=1, keepdims=True)
    lower = bounds_ref[0]
    upper = bounds_ref[1]
    restricted = (upper - lower) < GRID
    below = lax.broadcasted_iota(jnp.int32, (dims, dims), 0) > lax.broadcasted_iota(
        jnp.int32, (dims, dims), 1
    )
    rank = dot(
        jnp.where(below, 1.0, 0.0).astype(BF16),
        jnp.where(restricted, 1.0, 0.0).astype(BF16),
        1,
        0,
    )
    dim_ids = lax.broadcasted_iota(jnp.int32, (dims, 128), 0).astype(F32)
    scaled_upper = upper.astype(F32) * inverse
    scaled_lower = lower.astype(F32) * inverse
    rows = []
    for k in range(3):
        mine = restricted & (rank == float(k))
        for values in (scaled_upper, scaled_lower, dim_ids):
            rows.append(
                jnp.sum(jnp.where(mine, values, 0.0), axis=0, keepdims=True)
            )
    rows.append(counts_ref[...].astype(F32))
    rows.append(jnp.zeros((6, 128), F32))
    table[z_hi] = jnp.concatenate(rows, axis=0)

    pl.semaphore_wait(barrier, len(peers))

    copies = []
    a_copies = [
        send(pieces.at[y, a], pieces.at[y, a], a_sems, i - 1, at_a(i))
        for i in range(1, n_a)
    ]
    table_copy = send(table.at[z_hi], table.at[z_hi], table_sems, 0, partner)

    sums[...] = jnp.zeros_like(sums)

    def hot_rows(half):
        values = table[half]
        return [
            jnp.where(dim_ids == values[3 * k + 2 : 3 * k + 3], 1.0, 0.0)
            for k in range(3)
        ]

    def choose(half):
        values = table[half]
        hots = hot_rows(half)
        free = 1.0 - (hots[0] + hots[1] + hots[2])
        nothing = jnp.zeros((3 * dims, 128), BF16)
        pad = jnp.zeros((13, 128), F32)
        for k in range(3):
            minus = -hots[k].astype(BF16)
            for side in range(2):
                edge = values[3 * k + side : 3 * k + side + 1]
                high = edge.astype(BF16).astype(F32)
                middle = (edge - high).astype(BF16).astype(F32)
                low = edge - high - middle
                ends = jnp.concatenate([high, middle, low, pad], axis=0)
                column = (2 * k + side) * 128
                chosen[half, :, column : column + 128] = jnp.concatenate(
                    [minus, minus, minus, nothing, ends.astype(BF16)], axis=0
                )
        free = free.astype(BF16)
        offset = jnp.concatenate(
            [jnp.full((1, 128), -3.0, F32), jnp.zeros((15, 128), F32)], axis=0
        )
        chosen[half, :, 6 * 128 :] = jnp.concatenate(
            [nothing, free, free, free, offset.astype(BF16)], axis=0
        )

    choose(z_hi)
    row = lax.broadcasted_iota(jnp.int32, (16, width), 0)
    ones = jnp.where(row < 3, 1.0, 0.0).astype(BF16)

    def prepare(chunk):
        tiles = [pieces[chunk, i] for i in range(n_a)]
        step = samples_ref.shape[1]
        points = jnp.concatenate(
            [
                jnp.concatenate(
                    [t[:, step * i : step * i + step] for t in tiles], axis=1
                )
                for i in range(dims // 8)
            ],
            axis=0,
        )
        v_low = -points * inverse
        v_high = float(GRID) * inverse + v_low
        erf_high, moment_high = erf_and_moment(v_high)
        erf_low, moment_low = erf_and_moment(v_low)
        double_mass = erf_high - erf_low
        slopes[chunk] = (moment_low - moment_high) / double_mass
        logs = jnp.log(0.5 * double_mass) * LOG2E
        return jnp.concatenate(
            list(split3(-v_low)) + list(split3(logs)) + [ones], axis=0
        )

    def work(chunk, half, right):
        args[...] = dot(chosen[half], right, 0, 0)

        def tile(i, carry):
            start = pl.multiple_of(i * 8, 8)
            masses, moments = [], []
            for k in range(3):
                erf_high, moment_high = erf_and_moment(
                    args[pl.ds(start + 2 * k * 128, 8), :]
                )
                erf_low, moment_low = erf_and_moment(
                    args[pl.ds(start + (2 * k + 1) * 128, 8), :]
                )
                masses.append(erf_high - erf_low)
                moments.append(moment_low - moment_high)
            rest = jnp.exp2(args[pl.ds(start + 6 * 128, 8), :])
            rest0 = rest * masses[0]
            rest01 = rest0 * masses[1]
            within = rest01 * masses[2]
            inside[chunk, half, pl.ds(start, 8), :] = within
            parts = [
                within,
                rest * (masses[1] * masses[2]) * moments[0],
                rest0 * masses[2] * moments[1],
                rest01 * moments[2],
            ]
            for n, part in enumerate(parts):
                folded = part[:, :128]
                for j in range(1, width // 128):
                    folded = folded + part[:, 128 * j : 128 * j + 128]
                sums[n, half, pl.ds(start, 8), :] += folded
            return carry

        lax.fori_loop(0, 128 // 8, tile, 0, unroll=2)

    for copy in a_copies:
        copy.wait_recv()
    y_copies = [
        send(pieces.at[y], pieces.at[y], y_sems, i - 1, at_y(i)) for i in range(1, n_y)
    ]
    right = prepare(y)
    work(y, z_hi, right)
    table_copy.wait_recv()
    choose(1 - z_hi)
    work(y, 1 - z_hi, right)
    for i in range(1, n_y):
        y_copies[i - 1].wait_recv()
        chunk = (y + n_y - i) % n_y
        right = prepare(chunk)
        work(chunk, z_hi, right)
        work(chunk, 1 - z_hi, right)

    for half in range(n_hi):
        est[z, half : half + 1] = row_sums(sums[0, half])
    est_copies = [
        send(est.at[z], est.at[z], est_sems, i - 1, at_z(i)) for i in range(1, n_z)
    ]
    derivs = []
    for half in range(n_hi):
        hots = hot_rows(half)
        free = 1.0 - (hots[0] + hots[1] + hots[2])
        total = jnp.zeros((dims, 128), F32)
        for chunk in range(n_y):
            steep, steep_rest, _ = split3(slopes[chunk])
            within, within_rest, _ = split3(inside[chunk, half])
            total = total + dot(steep, within, 1, 1)
            total = total + dot(steep_rest, within, 1, 1)
            total = total + dot(steep, within_rest, 1, 1)
        total = total * free
        for k in range(3):
            total = total + hots[k] * row_sums(sums[k + 1, half])
        derivs.append(total)
    for copy in est_copies:
        copy.wait_recv()
    smoothing = 1.0 / TABLE_ROWS
    estimate = est[0]
    for i in range(1, n_z):
        estimate = estimate + est[i]
    estimate = estimate / sample_total
    counts = jnp.concatenate([table[half][9:10] for half in range(n_hi)], axis=0)
    log_est = jnp.log(estimate + smoothing)
    target = jnp.log(counts / TABLE_ROWS + smoothing)
    weight = 2.0 * (log_est - target) / (query_total * (estimate + smoothing))
    log_ref[...] = jnp.where(z_hi == 0, log_est[0:1], log_est[1:2])
    weighted = derivs[0] * weight[0:1]
    for half in range(1, n_hi):
        weighted = weighted + derivs[half] * weight[half : half + 1]
    weighted = jnp.concatenate([weighted, jnp.zeros((128 - dims, 128), F32)], axis=0)
    share = row_sums(weighted) * (SLOPE_SCALE / sample_total)

    def reduce_over(value, buffer, sems, place, peers):
        buffer[place] = value
        started = [
            send(buffer.at[place], buffer.at[place], sems, i, peer)
            for i, peer in enumerate(peers)
        ]
        for copy in started:
            copy.wait_recv()
        total = buffer[0]
        for i in range(1, buffer.shape[0]):
            total = total + buffer[i]
        return total, started

    share, gz = reduce_over(
        share, grad_z, gz_sems, z, [at_z(i) for i in range(1, n_z)]
    )
    share, ga = reduce_over(
        share, grad_a, ga_sems, a, [at_a(i) for i in range(1, n_a)]
    )
    share, gy = reduce_over(
        share, grad_y, gy_sems, y, [at_y(i) for i in range(1, n_y)]
    )
    grad_ref[...] = share[:, :dims]
    for copy in a_copies + [table_copy] + y_copies + est_copies + gz + ga + gy:
        copy.wait_send()


def on_device(sizes, samples, bounds, spread, counts):
    n_hi, n_y, n_a, n_lo = sizes
    n_z = n_hi * n_lo
    dims, local = samples.shape
    width = local * n_a
    queries = bounds.shape[2]
    sample_total = local * n_hi * n_y * n_a * n_lo
    query_total = queries * n_hi * n_y * n_a
    vmem = pl.BlockSpec(memory_space=pltpu.VMEM)
    dma = pltpu.SemaphoreType.DMA
    log_est, grad = pl.pallas_call(
        functools.partial(kernel, sizes, float(sample_total), float(query_total)),
        out_shape=(
            jax.ShapeDtypeStruct((1, queries), F32),
            jax.ShapeDtypeStruct((1, dims), F32),
        ),
        in_specs=[vmem] * 4,
        out_specs=(vmem, vmem),
        scratch_shapes=[
            pltpu.VMEM((n_hi, 16, 128), F32),
            pltpu.VMEM((n_y, n_a, 8, 128), F32),
            pltpu.VMEM((n_hi, DEPTH, ROWS_PER_HALF), BF16),
            pltpu.VMEM((ROWS_PER_HALF, width), F32),
            pltpu.VMEM((n_y, n_hi, 128, width), F32),
            pltpu.VMEM((n_y, dims, width), F32),
            pltpu.VMEM((4, n_hi, 128, 128), F32),
            pltpu.VMEM((n_z, n_hi, 128), F32),
            pltpu.VMEM((n_z, 1, 128), F32),
            pltpu.VMEM((n_a, 1, 128), F32),
            pltpu.VMEM((n_y, 1, 128), F32),
            dma((2, 1)),
            dma((2, n_a - 1)),
            dma((2, n_y - 1)),
            dma((2, n_z - 1)),
            dma((2, n_z - 1)),
            dma((2, n_a - 1)),
            dma((2, n_y - 1)),
        ],
        compiler_params=pltpu.CompilerParams(
            collective_id=0, has_side_effects=True, vmem_limit_bytes=40 * 1024 * 1024
        ),
    )(samples, bounds, spread.reshape(1, dims), counts.reshape(1, queries))
    return log_est.reshape(queries), grad.reshape(dims)


def solution(mesh):
    n_blk = mesh.shape["blk"]
    sizes = (2, 4, n_blk // 8, mesh.shape["grp"])
    return jax.shard_map(
        functools.partial(on_device, sizes),
        mesh=mesh,
        in_specs=(P(None, ("blk", "grp")), P(None, None, "blk"), P(), P("blk")),
        out_specs=(P("blk"), P()),
        check_vma=False,
    )
```

```python
import functools
import math

import jax
import jax.numpy as jnp
from jax import lax
from jax.experimental import pallas as pl
from jax.experimental.pallas import tpu as pltpu
from jax.sharding import PartitionSpec as P

TABLE_ROWS = 1048576
MESH = pl.DeviceIdType.MESH
F32 = jnp.float32
BF16 = jnp.bfloat16

UNIT = math.sqrt(math.log2(math.e) / 2.0)
LOG2E = math.log2(math.e)
ERF_COEFS = (
    0.939437726891315,
    0.059304200409920856,
    -7.37546114627212e-05,
    -0.00017348738576916883,
    1.7241095109019066e-05,
    -7.97342195757559e-07,
    1.4676678471795133e-08,
)
SLOPE_SCALE = 2.0 / (math.sqrt(2.0 * math.pi) * UNIT)

GRID = 256
ROWS_PER_HALF = 7 * 128
DEPTH = 208


def erf_and_moment(v):
    w = v * v
    poly = jnp.full_like(w, ERF_COEFS[-1])
    for coef in ERF_COEFS[-2::-1]:
        poly = poly * w + coef
    return jnp.tanh(v * poly), v * jnp.exp2(-w)


def split3(x):
    high = x.astype(BF16)
    rest = x - high.astype(F32)
    middle = rest.astype(BF16)
    low = (rest - middle.astype(F32)).astype(BF16)
    return high, middle, low


def dot(a, b, a_dim, b_dim):
    return lax.dot_general(
        a, b, (((a_dim,), (b_dim,)), ((), ())), preferred_element_type=F32
    )


def row_sums(x):
    pieces = jnp.concatenate(split3(x), axis=1)
    return dot(jnp.ones((8, pieces.shape[1]), BF16), pieces, 1, 1)[:1]


def kernel(
    sizes,
    sample_total,
    query_total,
    samples_hbm,
    bounds_hbm,
    spread_hbm,
    counts_hbm,
    log_ref,
    grad_ref,
    samples_ref,
    bounds_ref,
    spread_ref,
    counts_ref,
    table,
    pieces,
    rights,
    chosen,
    args,
    inside,
    slopes,
    sums,
    est,
    grad_z,
    grad_p,
    input_sems,
    table_sems,
    piece_sends,
    piece_recvs,
    est_sems,
    gz_sems,
    gp_sems,
):
    n_hi, n_y, n_a, n_lo = sizes
    n_z = n_hi * n_lo
    n_p = n_y * n_a
    dims, local = samples_ref.shape
    width = local * n_a

    inputs = []
    for i, (src, dst) in enumerate(
        (
            (samples_hbm, samples_ref),
            (spread_hbm, spread_ref),
            (bounds_hbm, bounds_ref),
            (counts_hbm, counts_ref),
        )
    ):
        copy = pltpu.make_async_copy(src, dst, input_sems.at[i])
        copy.start()
        inputs.append(copy)

    blk = lax.axis_index("blk")
    z_lo = lax.axis_index("grp")
    z_hi = blk // n_p
    plane = blk % n_p
    y = plane // n_a
    a = plane % n_a
    z = z_hi * n_lo + z_lo

    def at_z(step):
        other = (z + step) % n_z
        return ((other // n_lo) * n_p + plane, other % n_lo)

    def at_p(y_step, a_step):
        return (z_hi * n_p + ((y + y_step) % n_y) * n_a + (a + a_step) % n_a, z_lo)

    partner = ((1 - z_hi) * n_p + plane, z_lo)
    plane_steps = [(i, j) for i in range(n_y) for j in range(n_a) if i or j]

    barrier = pltpu.get_barrier_semaphore()
    peers = [at_p(i, j) for i, j in plane_steps]
    peers += [at_z(i) for i in range(1, n_z)]
    for peer in peers:
        pl.semaphore_signal(barrier, inc=1, device_id=peer, device_id_type=MESH)

    def send(ref, send_sem, recv_sem, peer):
        copy = pltpu.make_async_remote_copy(
            src_ref=ref,
            dst_ref=ref,
            send_sem=send_sem,
            recv_sem=recv_sem,
            device_id=peer,
            device_id_type=MESH,
        )
        copy.start()
        return copy

    def wait_bytes(ref, sem):
        pltpu.make_async_copy(ref, ref, sem).wait()

    inputs[0].wait()
    x = samples_ref[...]
    pieces[plane] = jnp.concatenate(
        [x[8 * i : 8 * i + 8] for i in range(dims // 8)], axis=1
    )
    pl.semaphore_wait(barrier, len(peers))
    for i, j in plane_steps:
        send(pieces.at[plane], piece_sends.at[0], piece_recvs.at[i], at_p(i, j))

    inputs[1].wait()
    inverse = UNIT / spread_ref[...]
    eye = lax.broadcasted_iota(jnp.int32, (dims, dims), 0) == lax.broadcasted_iota(
        jnp.int32, (dims, dims), 1
    )
    inverse = jnp.sum(jnp.where(eye, inverse, 0.0), axis=1, keepdims=True)
    inputs[2].wait()
    inputs[3].wait()
    lower = bounds_ref[0]
    upper = bounds_ref[1]
    restricted = (upper - lower) < GRID
    below = lax.broadcasted_iota(jnp.int32, (dims, dims), 0) > lax.broadcasted_iota(
        jnp.int32, (dims, dims), 1
    )
    rank = dot(
        jnp.where(below, 1.0, 0.0).astype(BF16),
        jnp.where(restricted, 1.0, 0.0).astype(BF16),
        1,
        0,
    )
    dim_ids = lax.broadcasted_iota(jnp.int32, (dims, 128), 0).astype(F32)
    scaled_upper = upper.astype(F32) * inverse
    scaled_lower = lower.astype(F32) * inverse
    rows = []
    for k in range(3):
        mine = restricted & (rank == float(k))
        for values in (scaled_upper, scaled_lower, dim_ids):
            rows.append(
                jnp.sum(jnp.where(mine, values, 0.0), axis=0, keepdims=True)
            )
    rows.append(counts_ref[...].astype(F32))
    rows.append(jnp.zeros((6, 128), F32))
    table[z_hi] = jnp.concatenate(rows, axis=0)
    table_copy = send(table.at[z_hi], table_sems.at[0], table_sems.at[1], partner)

    sums[...] = jnp.zeros_like(sums)

    def hot_rows(half):
        values = table[half]
        return [
            jnp.where(dim_ids == values[3 * k + 2 : 3 * k + 3], 1.0, 0.0)
            for k in range(3)
        ]

    def choose(half):
        values = table[half]
        hots = hot_rows(half)
        free = 1.0 - (hots[0] + hots[1] + hots[2])
        nothing = jnp.zeros((3 * dims, 128), BF16)
        pad = jnp.zeros((13, 128), F32)
        for k in range(3):
            minus = -hots[k].astype(BF16)
            for side in range(2):
                edge = values[3 * k + side : 3 * k + side + 1]
                high = edge.astype(BF16).astype(F32)
                middle = (edge - high).astype(BF16).astype(F32)
                low = edge - high - middle
                ends = jnp.concatenate([high, middle, low, pad], axis=0)
                column = (2 * k + side) * 128
                chosen[half, :, column : column + 128] = jnp.concatenate(
                    [minus, minus, minus, nothing, ends.astype(BF16)], axis=0
                )
        free = free.astype(BF16)
        offset = jnp.concatenate(
            [jnp.full((1, 128), -3.0, F32), jnp.zeros((15, 128), F32)], axis=0
        )
        chosen[half, :, 6 * 128 :] = jnp.concatenate(
            [nothing, free, free, free, offset.astype(BF16)], axis=0
        )

    choose(z_hi)
    row = lax.broadcasted_iota(jnp.int32, (16, width), 0)
    ones = jnp.where(row < 3, 1.0, 0.0).astype(BF16)

    def prepare(chunk):
        tiles = [pieces[chunk * n_a + i] for i in range(n_a)]
        points = jnp.concatenate(
            [
                jnp.concatenate(
                    [t[:, local * i : local * i + local] for t in tiles], axis=1
                )
                for i in range(dims // 8)
            ],
            axis=0,
        )
        v_low = -points * inverse
        v_high = float(GRID) * inverse + v_low
        erf_high, moment_high = erf_and_moment(v_high)
        erf_low, moment_low = erf_and_moment(v_low)
        double_mass = erf_high - erf_low
        slopes[chunk] = (moment_low - moment_high) / double_mass
        logs = jnp.log(0.5 * double_mass) * LOG2E
        rights[chunk] = jnp.concatenate(
            list(split3(-v_low)) + list(split3(logs)) + [ones], axis=0
        )

    def block(step, carry):
        i = step % n_y
        chunk = (y + n_y - i) % n_y

        @pl.when(step == 0)
        def _():
            wait_bytes(pieces.at[0 : n_a - 1], piece_recvs.at[i])

        @pl.when((step > 0) & (step < n_y))
        def _():
            wait_bytes(pieces.at[0:n_a], piece_recvs.at[i])

        @pl.when(step < n_y)
        def _():
            prepare(chunk)

        @pl.when(step == n_y)
        def _():
            table_copy.wait_recv()
            choose(1 - z_hi)

        half = jnp.where(step < n_y, z_hi, 1 - z_hi)
        args[...] = dot(chosen[half], rights[chunk], 0, 0)
        for start in range(0, 128, 8):
            masses, moments = [], []
            for k in range(3):
                base = start + 2 * k * 128
                erf_high, moment_high = erf_and_moment(args[base : base + 8, :])
                base = base + 128
                erf_low, moment_low = erf_and_moment(args[base : base + 8, :])
                masses.append(erf_high - erf_low)
                moments.append(moment_low - moment_high)
            rest = jnp.exp2(args[start + 6 * 128 : start + 6 * 128 + 8, :])
            rest0 = rest * masses[0]
            rest01 = rest0 * masses[1]
            within = rest01 * masses[2]
            inside[chunk, half, start : start + 8, :] = within
            parts = [
                within,
                rest * (masses[1] * masses[2]) * moments[0],
                rest0 * masses[2] * moments[1],
                rest01 * moments[2],
            ]
            for n, part in enumerate(parts):
                folded = part[:, :128]
                for j in range(1, width // 128):
                    folded = folded + part[:, 128 * j : 128 * j + 128]
                sums[n, half, start : start + 8, :] += folded
        return carry

    lax.fori_loop(0, n_hi * n_y, block, 0)

    for half in range(n_hi):
        est[z, half : half + 1] = row_sums(sums[0, half])
    for i in range(1, n_z):
        send(est.at[z], est_sems.at[0], est_sems.at[1], at_z(i))
    derivs = []
    for half in range(n_hi):
        hots = hot_rows(half)
        free = 1.0 - (hots[0] + hots[1] + hots[2])
        total = jnp.zeros((dims, 128), F32)
        for chunk in range(n_y):
            steep, steep_rest, _ = split3(slopes[chunk])
            within, within_rest, _ = split3(inside[chunk, half])
            total = total + dot(steep, within, 1, 1)
            total = total + dot(steep_rest, within, 1, 1)
            total = total + dot(steep, within_rest, 1, 1)
        total = total * free
        for k in range(3):
            total = total + hots[k] * row_sums(sums[k + 1, half])
        derivs.append(total)
    smoothing = 1.0 / TABLE_ROWS
    counts = jnp.concatenate([table[half][9:10] for half in range(n_hi)], axis=0)
    target = jnp.log(counts / TABLE_ROWS + smoothing)
    wait_bytes(est.at[0 : n_z - 1], est_sems.at[1])
    estimate = est[0]
    for i in range(1, n_z):
        estimate = estimate + est[i]
    estimate = estimate / sample_total
    log_est = jnp.log(estimate + smoothing)
    weight = 2.0 * (log_est - target) / (query_total * (estimate + smoothing))
    weighted = derivs[0] * weight[0:1]
    for half in range(1, n_hi):
        weighted = weighted + derivs[half] * weight[half : half + 1]
    weighted = jnp.concatenate([weighted, jnp.zeros((128 - dims, 128), F32)], axis=0)
    share = row_sums(weighted) * (SLOPE_SCALE / sample_total)

    grad_z[z] = share
    for i in range(1, n_z):
        send(grad_z.at[z], gz_sems.at[0], gz_sems.at[1], at_z(i))
    log_ref[...] = jnp.where(z_hi == 0, log_est[0:1], log_est[1:2])
    wait_bytes(grad_z.at[0 : n_z - 1], gz_sems.at[1])
    share = grad_z[0]
    for i in range(1, n_z):
        share = share + grad_z[i]
    grad_p[plane] = share
    for i, j in plane_steps:
        send(grad_p.at[plane], gp_sems.at[0], gp_sems.at[1], at_p(i, j))
    table_copy.wait_send()
    flat = n_p - 1
    wait_bytes(pieces.at[0:flat], piece_sends.at[0])
    wait_bytes(est.at[0 : n_z - 1], est_sems.at[0])
    wait_bytes(grad_z.at[0 : n_z - 1], gz_sems.at[0])
    wait_bytes(grad_p.at[0:flat], gp_sems.at[1])
    share = grad_p[0]
    for i in range(1, n_p):
        share = share + grad_p[i]
    grad_ref[...] = share[:, :dims]
    wait_bytes(grad_p.at[0:flat], gp_sems.at[0])


def on_device(sizes, samples, bounds, spread, counts):
    n_hi, n_y, n_a, n_lo = sizes
    n_z = n_hi * n_lo
    dims, local = samples.shape
    width = local * n_a
    queries = bounds.shape[2]
    sample_total = local * n_hi * n_y * n_a * n_lo
    query_total = queries * n_hi * n_y * n_a
    vmem = pl.BlockSpec(memory_space=pltpu.VMEM)
    whole = pl.BlockSpec(memory_space=pl.ANY)
    dma = pltpu.SemaphoreType.DMA
    log_est, grad = pl.pallas_call(
        functools.partial(kernel, sizes, float(sample_total), float(query_total)),
        out_shape=(
            jax.ShapeDtypeStruct((1, queries), F32),
            jax.ShapeDtypeStruct((1, dims), F32),
        ),
        in_specs=[whole] * 4,
        out_specs=(vmem, vmem),
        scratch_shapes=[
            pltpu.VMEM((dims, local), F32),
            pltpu.VMEM((2, dims, queries), jnp.int32),
            pltpu.VMEM((1, dims), F32),
            pltpu.VMEM((1, queries), jnp.int32),
            pltpu.VMEM((n_hi, 16, 128), F32),
            pltpu.VMEM((n_y * n_a, 8, 128), F32),
            pltpu.VMEM((n_y, DEPTH, width), BF16),
            pltpu.VMEM((n_hi, DEPTH, ROWS_PER_HALF), BF16),
            pltpu.VMEM((ROWS_PER_HALF, width), F32),
            pltpu.VMEM((n_y, n_hi, 128, width), F32),
            pltpu.VMEM((n_y, dims, width), F32),
            pltpu.VMEM((4, n_hi, 128, 128), F32),
            pltpu.VMEM((n_z, n_hi, 128), F32),
            pltpu.VMEM((n_z, 1, 128), F32),
            pltpu.VMEM((n_y * n_a, 1, 128), F32),
            dma((4,)),
            dma((2,)),
            dma((1,)),
            dma((n_y,)),
            dma((2,)),
            dma((2,)),
            dma((2,)),
        ],
        compiler_params=pltpu.CompilerParams(
            collective_id=0, has_side_effects=True, vmem_limit_bytes=40 * 1024 * 1024
        ),
    )(samples, bounds, spread.reshape(1, dims), counts.reshape(1, queries))
    return log_est.reshape(queries), grad.reshape(dims)


def solution(mesh):
    n_blk = mesh.shape["blk"]
    sizes = (2, 4, n_blk // 8, mesh.shape["grp"])
    return jax.shard_map(
        functools.partial(on_device, sizes),
        mesh=mesh,
        in_specs=(P(None, ("blk", "grp")), P(None, None, "blk"), P(), P("blk")),
        out_specs=(P("blk"), P()),
        check_vma=False,
    )
```

```python
import functools
import math

import jax
import jax.numpy as jnp
from jax import lax
from jax.experimental import pallas as pl
from jax.experimental.pallas import tpu as pltpu
from jax.sharding import PartitionSpec as P

TABLE_ROWS = 1048576
MESH = pl.DeviceIdType.MESH
F32 = jnp.float32
BF16 = jnp.bfloat16

UNIT = math.sqrt(math.log2(math.e) / 2.0)
LOG2E = math.log2(math.e)
ERF_COEFS = (
    0.939437726891315,
    0.059304200409920856,
    -7.37546114627212e-05,
    -0.00017348738576916883,
    1.7241095109019066e-05,
    -7.97342195757559e-07,
    1.4676678471795133e-08,
)
SLOPE_SCALE = 2.0 / (math.sqrt(2.0 * math.pi) * UNIT)

GRID = 256
GROUP = 16
REACH = 4
DEPTH = 208


def erf_and_moment(v):
    w = v * v
    poly = jnp.full_like(w, ERF_COEFS[-1])
    for coef in ERF_COEFS[-2::-1]:
        poly = poly * w + coef
    return jnp.tanh(v * poly), v * jnp.exp2(-w)


def split3(x):
    high = x.astype(BF16)
    rest = x - high.astype(F32)
    middle = rest.astype(BF16)
    low = (rest - middle.astype(F32)).astype(BF16)
    return high, middle, low


def dot(a, b, a_dim, b_dim):
    return lax.dot_general(
        a, b, (((a_dim,), (b_dim,)), ((), ())), preferred_element_type=F32
    )


def row_sums(x):
    pieces = jnp.concatenate(split3(x), axis=1)
    return dot(jnp.ones((8, pieces.shape[1]), BF16), pieces, 1, 1)[:1]


def kernel(
    sizes,
    sample_total,
    query_total,
    samples_hbm,
    bounds_hbm,
    spread_hbm,
    counts_hbm,
    log_ref,
    grad_ref,
    samples_ref,
    bounds_ref,
    spread_ref,
    counts_ref,
    table,
    pieces,
    rights,
    chosen,
    inside,
    slopes,
    sums,
    est,
    grad_z,
    grad_p,
    input_sems,
    table_sems,
    piece_sends,
    piece_recvs,
    est_sems,
    gz_sems,
    gp_sems,
    ready,
):
    n_hi, n_y, n_a, n_lo = sizes
    n_z = n_hi * n_lo
    n_p = n_y * n_a
    dims, local = samples_ref.shape
    width = local * n_a

    inputs = []
    for i, (src, dst) in enumerate(
        (
            (samples_hbm, samples_ref),
            (spread_hbm, spread_ref),
            (bounds_hbm, bounds_ref),
            (counts_hbm, counts_ref),
        )
    ):
        copy = pltpu.make_async_copy(src, dst, input_sems.at[i])
        copy.start()
        inputs.append(copy)

    blk = lax.axis_index("blk")
    z_lo = lax.axis_index("grp")
    z_hi = blk // n_p
    plane = blk % n_p
    y = plane // n_a
    a = plane % n_a
    z = z_hi * n_lo + z_lo

    def at_z(step):
        other = (z + step) % n_z
        return ((other // n_lo) * n_p + plane, other % n_lo)

    def at_p(y_step, a_step):
        return (z_hi * n_p + ((y + y_step) % n_y) * n_a + (a + a_step) % n_a, z_lo)

    partner = ((1 - z_hi) * n_p + plane, (z_lo + n_lo // 2) % n_lo)
    plane_steps = [(i, j) for i in range(n_y) for j in range(n_a) if i or j]

    barrier = pltpu.get_barrier_semaphore()
    peers = [at_p(i, j) for i, j in plane_steps]
    near = [i for i in range(1, n_z) if min(i, n_z - i) <= REACH]
    hubs = [i for i in near if min(i, n_z - i) == REACH]
    peers += [at_z(i) for i in near]
    for peer in peers:
        pl.semaphore_signal(barrier, inc=1, device_id=peer, device_id_type=MESH)

    def send(ref, send_sem, recv_sem, peer):
        copy = pltpu.make_async_remote_copy(
            src_ref=ref,
            dst_ref=ref,
            send_sem=send_sem,
            recv_sem=recv_sem,
            device_id=peer,
            device_id_type=MESH,
        )
        copy.start()
        return copy

    def wait_bytes(ref, sem):
        pltpu.make_async_copy(ref, ref, sem).wait()

    inputs[0].wait()
    x = samples_ref[...]
    pieces[plane] = jnp.concatenate(
        [x[8 * i : 8 * i + 8] for i in range(dims // 8)], axis=1
    )
    pl.semaphore_wait(barrier, len(peers))
    for i in hubs:
        pl.semaphore_signal(ready, inc=1, device_id=at_z(i), device_id_type=MESH)
    for i, j in plane_steps:
        send(pieces.at[plane], piece_sends.at[0], piece_recvs.at[i], at_p(i, j))

    inputs[1].wait()
    inverse = UNIT / spread_ref[...]
    eye = lax.broadcasted_iota(jnp.int32, (dims, dims), 0) == lax.broadcasted_iota(
        jnp.int32, (dims, dims), 1
    )
    inverse = jnp.sum(jnp.where(eye, inverse, 0.0), axis=1, keepdims=True)
    inputs[2].wait()
    inputs[3].wait()
    lower = bounds_ref[0]
    upper = bounds_ref[1]
    restricted = (upper - lower) < GRID
    below = lax.broadcasted_iota(jnp.int32, (dims, dims), 0) > lax.broadcasted_iota(
        jnp.int32, (dims, dims), 1
    )
    rank = dot(
        jnp.where(below, 1.0, 0.0).astype(BF16),
        jnp.where(restricted, 1.0, 0.0).astype(BF16),
        1,
        0,
    )
    dim_ids = lax.broadcasted_iota(jnp.int32, (dims, 128), 0).astype(F32)
    scaled_upper = upper.astype(F32) * inverse
    scaled_lower = lower.astype(F32) * inverse
    rows = []
    for k in range(3):
        mine = restricted & (rank == float(k))
        for values in (scaled_upper, scaled_lower, dim_ids):
            rows.append(
                jnp.sum(jnp.where(mine, values, 0.0), axis=0, keepdims=True)
            )
    rows.append(counts_ref[...].astype(F32))
    rows.append(jnp.zeros((6, 128), F32))
    table[z_hi] = jnp.concatenate(rows, axis=0)
    table_copy = send(table.at[z_hi], table_sems.at[0], table_sems.at[1], partner)

    sums[...] = jnp.zeros_like(sums)

    def hot_rows(half):
        values = table[half]
        return [
            jnp.where(dim_ids == values[3 * k + 2 : 3 * k + 3], 1.0, 0.0)
            for k in range(3)
        ]

    def choose(half):
        values = table[half]
        hots = hot_rows(half)
        free = 1.0 - (hots[0] + hots[1] + hots[2])
        nothing = jnp.zeros((3 * dims, 128), F32)
        pad = jnp.zeros((13, 128), F32)
        blocks = []
        for k in range(3):
            minus = -hots[k]
            for side in range(2):
                edge = values[3 * k + side : 3 * k + side + 1]
                high = edge.astype(BF16).astype(F32)
                middle = (edge - high).astype(BF16).astype(F32)
                low = edge - high - middle
                blocks.append([minus, minus, minus, nothing, high, middle, low, pad])
        offset = jnp.full((1, 128), -3.0, F32)
        none = jnp.zeros((15, 128), F32)
        blocks.append([nothing, free, free, free, offset, none])
        for n, block in enumerate(blocks):
            block = jnp.concatenate(block, axis=0).T.astype(BF16)
            for group in range(128 // GROUP):
                chosen[half, group, n * GROUP : n * GROUP + GROUP, :] = block[
                    group * GROUP : group * GROUP + GROUP
                ]

    choose(z_hi)
    row = lax.broadcasted_iota(jnp.int32, (16, width), 0)
    ones = jnp.where(row < 3, 1.0, 0.0).astype(BF16)

    def prepare(chunk):
        tiles = [pieces[chunk * n_a + i] for i in range(n_a)]
        points = jnp.concatenate(
            [
                jnp.concatenate(
                    [t[:, local * i : local * i + local] for t in tiles], axis=1
                )
                for i in range(dims // 8)
            ],
            axis=0,
        )
        v_low = -points * inverse
        v_high = float(GRID) * inverse + v_low
        erf_high, moment_high = erf_and_moment(v_high)
        erf_low, moment_low = erf_and_moment(v_low)
        double_mass = erf_high - erf_low
        slopes[chunk] = (moment_low - moment_high) / double_mass
        logs = jnp.log(0.5 * double_mass) * LOG2E
        rights[chunk] = jnp.concatenate(
            list(split3(-v_low)) + list(split3(logs)) + [ones], axis=0
        )

    def block(step, carry):
        i = step % n_y
        chunk = (y + n_y - i) % n_y

        @pl.when(step == 0)
        def _():
            wait_bytes(pieces.at[0 : n_a - 1], piece_recvs.at[i])

        @pl.when((step > 0) & (step < n_y))
        def _():
            wait_bytes(pieces.at[0:n_a], piece_recvs.at[i])

        @pl.when(step < n_y)
        def _():
            prepare(chunk)

        @pl.when(step == n_y)
        def _():
            table_copy.wait_recv()
            choose(1 - z_hi)

        half = jnp.where(step < n_y, z_hi, 1 - z_hi)
        right = rights[chunk]
        for group in range(128 // GROUP):
            terms = dot(chosen[half, group], right, 1, 0)
            terms = [terms[n * GROUP : n * GROUP + GROUP] for n in range(7)]
            start = group * GROUP
            masses, moments = [], []
            for k in range(3):
                erf_high, moment_high = erf_and_moment(terms[2 * k])
                erf_low, moment_low = erf_and_moment(terms[2 * k + 1])
                masses.append(erf_high - erf_low)
                moments.append(moment_low - moment_high)
            rest = jnp.exp2(terms[6])
            rest0 = rest * masses[0]
            rest01 = rest0 * masses[1]
            within = rest01 * masses[2]
            inside[chunk, half, start : start + GROUP, :] = within
            parts = [
                within,
                rest * (masses[1] * masses[2]) * moments[0],
                rest0 * masses[2] * moments[1],
                rest01 * moments[2],
            ]
            for n, part in enumerate(parts):
                folded = part[:, :128]
                for j in range(1, width // 128):
                    folded = folded + part[:, 128 * j : 128 * j + 128]
                sums[n, half, start : start + GROUP, :] += folded
        return carry

    lax.fori_loop(0, n_hi * n_y, block, 0)

    for half in range(n_hi):
        est[z, half : half + 1] = row_sums(sums[0, half])
    if hubs:
        pl.semaphore_wait(ready, len(hubs))
    for i in range(1, n_z):
        send(est.at[z], est_sems.at[0], est_sems.at[1], at_z(i))
    derivs = []
    for half in range(n_hi):
        hots = hot_rows(half)
        free = 1.0 - (hots[0] + hots[1] + hots[2])
        total = jnp.zeros((dims, 128), F32)
        for chunk in range(n_y):
            steep, steep_rest, _ = split3(slopes[chunk])
            within, within_rest, _ = split3(inside[chunk, half])
            total = total + dot(steep, within, 1, 1)
            total = total + dot(steep_rest, within, 1, 1)
            total = total + dot(steep, within_rest, 1, 1)
        total = total * free
        for k in range(3):
            total = total + hots[k] * row_sums(sums[k + 1, half])
        derivs.append(total)
    smoothing = 1.0 / TABLE_ROWS
    counts = jnp.concatenate([table[half][9:10] for half in range(n_hi)], axis=0)
    target = jnp.log(counts / TABLE_ROWS + smoothing)
    wait_bytes(est.at[0 : n_z - 1], est_sems.at[1])
    estimate = est[0]
    for i in range(1, n_z):
        estimate = estimate + est[i]
    estimate = estimate / sample_total
    log_est = jnp.log(estimate + smoothing)
    weight = 2.0 * (log_est - target) / (query_total * (estimate + smoothing))
    weighted = derivs[0] * weight[0:1]
    for half in range(1, n_hi):
        weighted = weighted + derivs[half] * weight[half : half + 1]
    weighted = jnp.concatenate([weighted, jnp.zeros((128 - dims, 128), F32)], axis=0)
    share = row_sums(weighted) * (SLOPE_SCALE / sample_total)

    grad_p[plane] = share
    for i, j in plane_steps:
        send(grad_p.at[plane], gp_sems.at[0], gp_sems.at[1], at_p(i, j))
    log_ref[...] = jnp.where(z_hi == 0, log_est[0:1], log_est[1:2])
    flat = n_p - 1
    wait_bytes(grad_p.at[0:flat], gp_sems.at[1])
    share = grad_p[0]
    for i in range(1, n_p):
        share = share + grad_p[i]
    grad_z[z] = share
    for i in range(1, n_z):
        send(grad_z.at[z], gz_sems.at[0], gz_sems.at[1], at_z(i))
    table_copy.wait_send()
    wait_bytes(pieces.at[0:flat], piece_sends.at[0])
    wait_bytes(est.at[0 : n_z - 1], est_sems.at[0])
    wait_bytes(grad_p.at[0:flat], gp_sems.at[0])
    wait_bytes(grad_z.at[0 : n_z - 1], gz_sems.at[1])
    share = grad_z[0]
    for i in range(1, n_z):
        share = share + grad_z[i]
    grad_ref[...] = share[:, :dims]
    wait_bytes(grad_z.at[0 : n_z - 1], gz_sems.at[0])


def on_device(sizes, samples, bounds, spread, counts):
    n_hi, n_y, n_a, n_lo = sizes
    n_z = n_hi * n_lo
    dims, local = samples.shape
    width = local * n_a
    queries = bounds.shape[2]
    sample_total = local * n_hi * n_y * n_a * n_lo
    query_total = queries * n_hi * n_y * n_a
    vmem = pl.BlockSpec(memory_space=pltpu.VMEM)
    whole = pl.BlockSpec(memory_space=pltpu.HBM)
    dma = pltpu.SemaphoreType.DMA
    inputs = [
        pltpu.with_memory_space_constraint(value, pltpu.HBM)
        for value in (
            samples,
            bounds,
            spread.reshape(1, dims),
            counts.reshape(1, queries),
        )
    ]
    log_est, grad = pl.pallas_call(
        functools.partial(kernel, sizes, float(sample_total), float(query_total)),
        out_shape=(
            jax.ShapeDtypeStruct((1, queries), F32),
            jax.ShapeDtypeStruct((1, dims), F32),
        ),
        in_specs=[whole] * 4,
        out_specs=(vmem, vmem),
        scratch_shapes=[
            pltpu.VMEM((dims, local), F32),
            pltpu.VMEM((2, dims, queries), jnp.int32),
            pltpu.VMEM((1, dims), F32),
            pltpu.VMEM((1, queries), jnp.int32),
            pltpu.VMEM((n_hi, 16, 128), F32),
            pltpu.VMEM((n_y * n_a, 8, 128), F32),
            pltpu.VMEM((n_y, DEPTH, width), BF16),
            pltpu.VMEM((n_hi, 128 // GROUP, 7 * GROUP, DEPTH), BF16),
            pltpu.VMEM((n_y, n_hi, 128, width), F32),
            pltpu.VMEM((n_y, dims, width), F32),
            pltpu.VMEM((4, n_hi, 128, 128), F32),
            pltpu.VMEM((n_z, n_hi, 128), F32),
            pltpu.VMEM((n_z, 1, 128), F32),
            pltpu.VMEM((n_y * n_a, 1, 128), F32),
            dma((4,)),
            dma((2,)),
            dma((1,)),
            dma((n_y,)),
            dma((2,)),
            dma((2,)),
            dma((2,)),
            pltpu.SemaphoreType.REGULAR,
        ],
        compiler_params=pltpu.CompilerParams(
            collective_id=0, has_side_effects=True, vmem_limit_bytes=40 * 1024 * 1024
        ),
    )(*inputs)
    return log_est.reshape(queries), grad.reshape(dims)


def solution(mesh):
    n_blk = mesh.shape["blk"]
    sizes = (2, 4, n_blk // 8, mesh.shape["grp"])
    return jax.shard_map(
        functools.partial(on_device, sizes),
        mesh=mesh,
        in_specs=(P(None, ("blk", "grp")), P(None, None, "blk"), P(), P("blk")),
        out_specs=(P("blk"), P()),
        check_vma=False,
    )
```

```python
import functools
import math

import jax
import jax.numpy as jnp
from jax import lax
from jax.experimental import pallas as pl
from jax.experimental.pallas import tpu as pltpu
from jax.sharding import PartitionSpec as P

TABLE_ROWS = 1048576
MESH = pl.DeviceIdType.MESH
F32 = jnp.float32
BF16 = jnp.bfloat16

UNIT = math.sqrt(math.log2(math.e) / 2.0)
LOG2E = math.log2(math.e)
ERF_COEFS = (
    0.939437726891315,
    0.059304200409920856,
    -7.37546114627212e-05,
    -0.00017348738576916883,
    1.7241095109019066e-05,
    -7.97342195757559e-07,
    1.4676678471795133e-08,
)
SLOPE_SCALE = 2.0 / (math.sqrt(2.0 * math.pi) * UNIT)

GRID = 256
GROUP = 16
REACH = 4
DEPTH = 208


def erf_of(v):
    w = v * v
    poly = ERF_COEFS[-1] * w + ERF_COEFS[-2]
    for coef in ERF_COEFS[-3::-1]:
        poly = poly * w + coef
    return jnp.tanh(v * poly)


def moment_of(v):
    return v * jnp.exp2(-(v * v))


def split3(x):
    high = x.astype(BF16)
    rest = x - high.astype(F32)
    middle = rest.astype(BF16)
    low = (rest - middle.astype(F32)).astype(BF16)
    return high, middle, low


def dot(a, b, a_dim, b_dim):
    return lax.dot_general(
        a, b, (((a_dim,), (b_dim,)), ((), ())), preferred_element_type=F32
    )


def row_sums(x):
    pieces = jnp.concatenate(split3(x), axis=1)
    return dot(jnp.ones((8, pieces.shape[1]), BF16), pieces, 1, 1)[:1]


def kernel(
    sizes,
    sample_total,
    query_total,
    samples_hbm,
    bounds_hbm,
    spread_hbm,
    counts_hbm,
    log_ref,
    grad_ref,
    samples_ref,
    bounds_ref,
    spread_ref,
    counts_ref,
    table,
    pieces,
    rights,
    chosen,
    inside,
    leaves,
    sums,
    est,
    grad_z,
    grad_p,
    input_sems,
    table_sems,
    piece_sends,
    piece_recvs,
    est_sems,
    gz_sems,
    gp_sems,
    ready,
):
    n_hi, n_y, n_a, n_lo = sizes
    n_z = n_hi * n_lo
    n_p = n_y * n_a
    dims, local = samples_ref.shape
    width = local * n_a

    inputs = []
    for i, (src, dst) in enumerate(
        (
            (samples_hbm, samples_ref),
            (spread_hbm, spread_ref),
            (bounds_hbm, bounds_ref),
            (counts_hbm, counts_ref),
        )
    ):
        copy = pltpu.make_async_copy(src, dst, input_sems.at[i])
        copy.start()
        inputs.append(copy)

    blk = lax.axis_index("blk")
    z_lo = lax.axis_index("grp")
    z_hi = blk // n_p
    plane = blk % n_p
    y = plane // n_a
    a = plane % n_a
    z = z_hi * n_lo + z_lo

    def at_z(step):
        other = (z + step) % n_z
        return ((other // n_lo) * n_p + plane, other % n_lo)

    def at_p(y_step, a_step):
        return (z_hi * n_p + ((y + y_step) % n_y) * n_a + (a + a_step) % n_a, z_lo)

    partner = ((1 - z_hi) * n_p + plane, (z_lo + n_lo // 2) % n_lo)
    plane_steps = sorted(
        ((i, j) for i in range(n_y) for j in range(n_a) if i or j),
        key=lambda s: -2 * min(s[0], n_y - s[0]) - min(s[1], n_a - s[1]),
    )
    z_steps = sorted(range(1, n_z), key=lambda i: -min(i, n_z - i))

    barrier = pltpu.get_barrier_semaphore()
    peers = []
    near = [i for i in z_steps if min(i, n_z - i) <= REACH]
    hubs = [i for i in near if min(i, n_z - i) == REACH]
    peers += [at_z(i) for i in near]
    peers += [at_p(i, j) for i, j in plane_steps]
    for peer in peers:
        pl.semaphore_signal(barrier, inc=1, device_id=peer, device_id_type=MESH)

    def send(ref, send_sem, recv_sem, peer):
        copy = pltpu.make_async_remote_copy(
            src_ref=ref,
            dst_ref=ref,
            send_sem=send_sem,
            recv_sem=recv_sem,
            device_id=peer,
            device_id_type=MESH,
        )
        copy.start()
        return copy

    def wait_bytes(ref, sem):
        pltpu.make_async_copy(ref, ref, sem).wait()

    inputs[0].wait()
    x = samples_ref[...]
    pieces[plane] = jnp.concatenate(
        [x[8 * i : 8 * i + 8] for i in range(dims // 8)], axis=1
    )
    pl.semaphore_wait(barrier, len(peers))
    for i in hubs:
        pl.semaphore_signal(ready, inc=1, device_id=at_z(i), device_id_type=MESH)
    for i, j in plane_steps:
        send(pieces.at[plane], piece_sends.at[0], piece_recvs.at[i], at_p(i, j))

    inputs[1].wait()
    inverse = UNIT / spread_ref[...]
    eye = lax.broadcasted_iota(jnp.int32, (dims, dims), 0) == lax.broadcasted_iota(
        jnp.int32, (dims, dims), 1
    )
    inverse = jnp.sum(jnp.where(eye, inverse, 0.0), axis=1, keepdims=True)
    inputs[2].wait()
    inputs[3].wait()
    lower = bounds_ref[0]
    upper = bounds_ref[1]
    restricted = (upper - lower) < GRID
    below = lax.broadcasted_iota(jnp.int32, (dims, dims), 0) > lax.broadcasted_iota(
        jnp.int32, (dims, dims), 1
    )
    rank = dot(
        jnp.where(below, 1.0, 0.0).astype(BF16),
        jnp.where(restricted, 1.0, 0.0).astype(BF16),
        1,
        0,
    )
    dim_ids = lax.broadcasted_iota(jnp.int32, (dims, 128), 0).astype(F32)
    scaled_upper = upper.astype(F32) * inverse
    scaled_lower = lower.astype(F32) * inverse
    rows = []
    for k in range(3):
        mine = restricted & (rank == float(k))
        for values in (scaled_upper, scaled_lower, dim_ids):
            rows.append(
                jnp.sum(jnp.where(mine, values, 0.0), axis=0, keepdims=True)
            )
    rows.append(counts_ref[...].astype(F32))
    rows.append(jnp.zeros((6, 128), F32))
    table[z_hi] = jnp.concatenate(rows, axis=0)
    table_copy = send(table.at[z_hi], table_sems.at[0], table_sems.at[1], partner)

    def hot_rows(half):
        values = table[half]
        return [
            jnp.where(dim_ids == values[3 * k + 2 : 3 * k + 3], 1.0, 0.0)
            for k in range(3)
        ]

    def choose(half):
        values = table[half]
        hots = hot_rows(half)
        free = 1.0 - (hots[0] + hots[1] + hots[2])
        nothing = jnp.zeros((3 * dims, 128), F32)
        pad = jnp.zeros((13, 128), F32)
        blocks = []
        for k in range(3):
            minus = -hots[k]
            for side in range(2):
                edge = values[3 * k + side : 3 * k + side + 1]
                high = edge.astype(BF16).astype(F32)
                middle = (edge - high).astype(BF16).astype(F32)
                low = edge - high - middle
                blocks.append([minus, minus, minus, nothing, high, middle, low, pad])
        offset = jnp.full((1, 128), -3.0, F32)
        none = jnp.zeros((15, 128), F32)
        blocks.append([nothing, free, free, free, offset, none])
        for n, block in enumerate(blocks):
            block = jnp.concatenate(block, axis=0).T.astype(BF16)
            for group in range(128 // GROUP):
                chosen[half, group, n * GROUP : n * GROUP + GROUP, :] = block[
                    group * GROUP : group * GROUP + GROUP
                ]

    choose(z_hi)
    row = lax.broadcasted_iota(jnp.int32, (16, width), 0)
    ones = jnp.where(row < 3, 1.0, 0.0).astype(BF16)

    def points_of(chunk):
        tiles = [pieces[chunk * n_a + i] for i in range(n_a)]
        points = jnp.concatenate(
            [
                jnp.concatenate(
                    [t[:, local * i : local * i + local] for t in tiles], axis=1
                )
                for i in range(dims // 8)
            ],
            axis=0,
        )
        return points * inverse

    def prepare(chunk):
        point = points_of(chunk)
        erf_high = erf_of(float(GRID) * inverse - point)
        mass = 0.5 * (erf_high + erf_of(point))
        logs = jnp.log(mass) * LOG2E
        rights[:, chunk * width : chunk * width + width] = jnp.concatenate(
            list(split3(point)) + list(split3(logs)) + [ones], axis=0
        )

    def slope_of(chunk):
        point = points_of(chunk)
        beyond = float(GRID) * inverse - point
        return -(moment_of(point) + moment_of(beyond)) / (erf_of(beyond) + erf_of(point))

    def arguments(half, group, chunk, rows):
        terms = dot(
            chosen[half, group, : rows * GROUP],
            rights[:, chunk * width : chunk * width + width],
            1,
            0,
        )
        return [terms[n * GROUP : n * GROUP + GROUP] for n in range(rows)]

    def fold(part):
        total = part[:, :128]
        for j in range(1, width // 128):
            total = total + part[:, 128 * j : 128 * j + 128]
        return total

    def masses_of(half):
        for group in range(128 // GROUP):
            here = slice(group * GROUP, group * GROUP + GROUP)
            total = None
            for chunk in range(n_y):
                terms = arguments(half, group, chunk, 7)
                first, second, third = (
                    erf_of(terms[2 * k]) - erf_of(terms[2 * k + 1]) for k in range(3)
                )
                rest = jnp.exp2(terms[6])
                rest0 = rest * first
                rest01 = rest0 * second
                within = rest01 * third
                inside[chunk, half, here, :] = within
                leaves[0, chunk, half, here, :] = rest * (second * third)
                leaves[1, chunk, half, here, :] = rest0 * third
                leaves[2, chunk, half, here, :] = rest01
                part = fold(within)
                total = part if total is None else total + part
            sums[0, half, here, :] = total

    def moments_of(half):
        for group in range(128 // GROUP):
            here = slice(group * GROUP, group * GROUP + GROUP)
            totals = [None] * 3
            for chunk in range(n_y):
                terms = arguments(half, group, chunk, 6)
                for k in range(3):
                    moment = moment_of(terms[2 * k + 1]) - moment_of(terms[2 * k])
                    part = fold(leaves[k, chunk, half, here, :] * moment)
                    totals[k] = part if totals[k] is None else totals[k] + part
            for k in range(3):
                sums[k + 1, half, here, :] = totals[k]

    for i in range(n_y):
        count = n_a - 1 if i == 0 else n_a
        wait_bytes(pieces.at[0:count], piece_recvs.at[i])
    for chunk in range(n_y):
        prepare(chunk)

    def half_block(step, carry):
        @pl.when(step == 1)
        def _():
            table_copy.wait_recv()
            choose(1 - z_hi)

        masses_of(jnp.where(step == 0, z_hi, 1 - z_hi))
        return carry

    lax.fori_loop(0, n_hi, half_block, 0)

    for half in range(n_hi):
        est[z, half : half + 1] = row_sums(sums[0, half])
    if hubs:
        pl.semaphore_wait(ready, len(hubs))
    for i in z_steps:
        send(est.at[z], est_sems.at[0], est_sems.at[1], at_z(i))
    def half_moments(half, carry):
        moments_of(half)
        return carry

    lax.fori_loop(0, n_hi, half_moments, 0)
    derivs = []
    slopes = [split3(slope_of(chunk)) for chunk in range(n_y)]
    for half in range(n_hi):
        hots = hot_rows(half)
        free = 1.0 - (hots[0] + hots[1] + hots[2])
        total = jnp.zeros((dims, 128), F32)
        for chunk in range(n_y):
            steep, steep_rest, _ = slopes[chunk]
            within, within_rest, _ = split3(inside[chunk, half])
            total = total + dot(steep, within, 1, 1)
            total = total + dot(steep_rest, within, 1, 1)
            total = total + dot(steep, within_rest, 1, 1)
        total = total * free
        for k in range(3):
            total = total + hots[k] * row_sums(sums[k + 1, half])
        derivs.append(total)
    smoothing = 1.0 / TABLE_ROWS
    counts = jnp.concatenate([table[half][9:10] for half in range(n_hi)], axis=0)
    target = jnp.log(counts / TABLE_ROWS + smoothing)
    wait_bytes(est.at[0 : n_z - 1], est_sems.at[1])
    estimate = est[0]
    for i in range(1, n_z):
        estimate = estimate + est[i]
    estimate = estimate / sample_total
    log_est = jnp.log(estimate + smoothing)
    weight = 2.0 * (log_est - target) / (query_total * (estimate + smoothing))
    weighted = derivs[0] * weight[0:1]
    for half in range(1, n_hi):
        weighted = weighted + derivs[half] * weight[half : half + 1]
    weighted = jnp.concatenate([weighted, jnp.zeros((128 - dims, 128), F32)], axis=0)
    share = row_sums(weighted) * (SLOPE_SCALE / sample_total)

    grad_p[plane] = share
    for i, j in plane_steps:
        send(grad_p.at[plane], gp_sems.at[0], gp_sems.at[1], at_p(i, j))
    log_ref[...] = jnp.where(z_hi == 0, log_est[0:1], log_est[1:2])
    flat = n_p - 1
    wait_bytes(grad_p.at[0:flat], gp_sems.at[1])
    share = grad_p[0]
    for i in range(1, n_p):
        share = share + grad_p[i]
    grad_z[z] = share
    for i in z_steps:
        send(grad_z.at[z], gz_sems.at[0], gz_sems.at[1], at_z(i))
    table_copy.wait_send()
    wait_bytes(pieces.at[0:flat], piece_sends.at[0])
    wait_bytes(est.at[0 : n_z - 1], est_sems.at[0])
    wait_bytes(grad_p.at[0:flat], gp_sems.at[0])
    wait_bytes(grad_z.at[0 : n_z - 1], gz_sems.at[1])
    share = grad_z[0]
    for i in range(1, n_z):
        share = share + grad_z[i]
    grad_ref[...] = share[:, :dims]
    wait_bytes(grad_z.at[0 : n_z - 1], gz_sems.at[0])


def on_device(sizes, samples, bounds, spread, counts):
    n_hi, n_y, n_a, n_lo = sizes
    n_z = n_hi * n_lo
    dims, local = samples.shape
    width = local * n_a
    queries = bounds.shape[2]
    sample_total = local * n_hi * n_y * n_a * n_lo
    query_total = queries * n_hi * n_y * n_a
    vmem = pl.BlockSpec(memory_space=pltpu.VMEM)
    whole = pl.BlockSpec(memory_space=pltpu.HBM)
    dma = pltpu.SemaphoreType.DMA
    inputs = [
        pltpu.with_memory_space_constraint(value, pltpu.HBM)
        for value in (
            samples,
            bounds,
            spread.reshape(1, dims),
            counts.reshape(1, queries),
        )
    ]
    log_est, grad = pl.pallas_call(
        functools.partial(kernel, sizes, float(sample_total), float(query_total)),
        out_shape=(
            jax.ShapeDtypeStruct((1, queries), F32),
            jax.ShapeDtypeStruct((1, dims), F32),
        ),
        in_specs=[whole] * 4,
        out_specs=(vmem, vmem),
        scratch_shapes=[
            pltpu.VMEM((dims, local), F32),
            pltpu.VMEM((2, dims, queries), jnp.int32),
            pltpu.VMEM((1, dims), F32),
            pltpu.VMEM((1, queries), jnp.int32),
            pltpu.VMEM((n_hi, 16, 128), F32),
            pltpu.VMEM((n_y * n_a, 8, 128), F32),
            pltpu.VMEM((DEPTH, n_y * width), BF16),
            pltpu.VMEM((n_hi, 128 // GROUP, 7 * GROUP, DEPTH), BF16),
            pltpu.VMEM((n_y, n_hi, 128, width), F32),
            pltpu.VMEM((3, n_y, n_hi, 128, width), F32),
            pltpu.VMEM((4, n_hi, 128, 128), F32),
            pltpu.VMEM((n_z, n_hi, 128), F32),
            pltpu.VMEM((n_z, 1, 128), F32),
            pltpu.VMEM((n_y * n_a, 1, 128), F32),
            dma((4,)),
            dma((2,)),
            dma((1,)),
            dma((n_y,)),
            dma((2,)),
            dma((2,)),
            dma((2,)),
            pltpu.SemaphoreType.REGULAR,
        ],
        compiler_params=pltpu.CompilerParams(
            collective_id=0, has_side_effects=True, vmem_limit_bytes=40 * 1024 * 1024
        ),
    )(*inputs)
    return log_est.reshape(queries), grad.reshape(dims)


def solution(mesh):
    n_blk = mesh.shape["blk"]
    sizes = (2, 4, n_blk // 8, mesh.shape["grp"])
    return jax.shard_map(
        functools.partial(on_device, sizes),
        mesh=mesh,
        in_specs=(P(None, ("blk", "grp")), P(None, None, "blk"), P(), P("blk")),
        out_specs=(P("blk"), P()),
        check_vma=False,
    )
```

```python
import functools
import math

import jax
import jax.numpy as jnp
from jax import lax
from jax.experimental import pallas as pl
from jax.experimental.pallas import tpu as pltpu
from jax.sharding import PartitionSpec as P

TABLE_ROWS = 1048576
MESH = pl.DeviceIdType.MESH
F32 = jnp.float32
BF16 = jnp.bfloat16

UNIT = math.sqrt(math.log2(math.e) / 2.0)
LOG2E = math.log2(math.e)
ERF_COEFS = (
    0.939437726891315,
    0.059304200409920856,
    -7.37546114627212e-05,
    -0.00017348738576916883,
    1.7241095109019066e-05,
    -7.97342195757559e-07,
    1.4676678471795133e-08,
)
SLOPE_SCALE = 2.0 / (math.sqrt(2.0 * math.pi) * UNIT)

GRID = 256
GROUP = 32
REACH = 4
DEPTH = 208


def erf_of(v):
    w = v * v
    poly = ERF_COEFS[-1] * w + ERF_COEFS[-2]
    for coef in ERF_COEFS[-3::-1]:
        poly = poly * w + coef
    return jnp.tanh(v * poly)


def moment_of(v):
    return v * jnp.exp2(-(v * v))


def split3(x):
    high = x.astype(BF16)
    rest = x - high.astype(F32)
    middle = rest.astype(BF16)
    low = (rest - middle.astype(F32)).astype(BF16)
    return high, middle, low


def dot(a, b, a_dim, b_dim):
    return lax.dot_general(
        a, b, (((a_dim,), (b_dim,)), ((), ())), preferred_element_type=F32
    )


def row_sums(x):
    pieces = jnp.concatenate(split3(x), axis=1)
    return dot(jnp.ones((8, pieces.shape[1]), BF16), pieces, 1, 1)[:1]


def kernel(
    sizes,
    sample_total,
    query_total,
    samples_hbm,
    bounds_hbm,
    spread_hbm,
    counts_hbm,
    log_ref,
    grad_ref,
    samples_ref,
    bounds_ref,
    spread_ref,
    counts_ref,
    table,
    pieces,
    rights,
    chosen,
    inside,
    leaves,
    sums,
    est,
    grad_z,
    grad_p,
    input_sems,
    table_sems,
    piece_sends,
    piece_recvs,
    est_sems,
    gz_sems,
    gp_sems,
    ready,
):
    n_hi, n_y, n_a, n_lo = sizes
    n_z = n_hi * n_lo
    n_p = n_y * n_a
    dims, local = samples_ref.shape
    width = local * n_a

    inputs = []
    for i, (src, dst) in enumerate(
        (
            (samples_hbm, samples_ref),
            (spread_hbm, spread_ref),
            (bounds_hbm, bounds_ref),
            (counts_hbm, counts_ref),
        )
    ):
        copy = pltpu.make_async_copy(src, dst, input_sems.at[i])
        copy.start()
        inputs.append(copy)

    blk = lax.axis_index("blk")
    z_lo = lax.axis_index("grp")
    z_hi = blk // n_p
    plane = blk % n_p
    y = plane // n_a
    a = plane % n_a
    z = z_hi * n_lo + z_lo

    def at_z(step):
        other = (z + step) % n_z
        return ((other // n_lo) * n_p + plane, other % n_lo)

    def at_p(y_step, a_step):
        return (z_hi * n_p + ((y + y_step) % n_y) * n_a + (a + a_step) % n_a, z_lo)

    partner = ((1 - z_hi) * n_p + plane, (z_lo + n_lo // 2) % n_lo)
    plane_steps = sorted(
        ((i, j) for i in range(n_y) for j in range(n_a) if i or j),
        key=lambda s: -2 * min(s[0], n_y - s[0]) - min(s[1], n_a - s[1]),
    )
    z_steps = sorted(range(1, n_z), key=lambda i: -min(i, n_z - i))

    barrier = pltpu.get_barrier_semaphore()
    peers = []
    near = [i for i in z_steps if min(i, n_z - i) <= REACH]
    hubs = [i for i in near if min(i, n_z - i) == REACH]
    peers += [at_z(i) for i in near]
    peers += [at_p(i, j) for i, j in plane_steps]
    for peer in peers:
        pl.semaphore_signal(barrier, inc=1, device_id=peer, device_id_type=MESH)

    def send(ref, send_sem, recv_sem, peer):
        copy = pltpu.make_async_remote_copy(
            src_ref=ref,
            dst_ref=ref,
            send_sem=send_sem,
            recv_sem=recv_sem,
            device_id=peer,
            device_id_type=MESH,
        )
        copy.start()
        return copy

    def wait_bytes(ref, sem):
        pltpu.make_async_copy(ref, ref, sem).wait()

    inputs[0].wait()
    x = samples_ref[...]
    pieces[plane] = jnp.concatenate(
        [x[8 * i : 8 * i + 8] for i in range(dims // 8)], axis=1
    )
    inputs[1].wait()
    inverse = UNIT / spread_ref[...]
    eye = lax.broadcasted_iota(jnp.int32, (dims, dims), 0) == lax.broadcasted_iota(
        jnp.int32, (dims, dims), 1
    )
    inverse = jnp.sum(jnp.where(eye, inverse, 0.0), axis=1, keepdims=True)
    inputs[2].wait()
    inputs[3].wait()
    lower = bounds_ref[0]
    upper = bounds_ref[1]
    restricted = (upper - lower) < GRID
    below = lax.broadcasted_iota(jnp.int32, (dims, dims), 0) > lax.broadcasted_iota(
        jnp.int32, (dims, dims), 1
    )
    rank = dot(
        jnp.where(below, 1.0, 0.0).astype(BF16),
        jnp.where(restricted, 1.0, 0.0).astype(BF16),
        1,
        0,
    )
    dim_ids = lax.broadcasted_iota(jnp.int32, (dims, 128), 0).astype(F32)
    scaled_upper = upper.astype(F32) * inverse
    scaled_lower = lower.astype(F32) * inverse
    rows = []
    for k in range(3):
        mine = restricted & (rank == float(k))
        for values in (scaled_upper, scaled_lower, dim_ids):
            rows.append(
                jnp.sum(jnp.where(mine, values, 0.0), axis=0, keepdims=True)
            )
    rows.append(counts_ref[...].astype(F32))
    rows.append(jnp.zeros((6, 128), F32))
    table[z_hi] = jnp.concatenate(rows, axis=0)
    def hot_rows(half):
        values = table[half]
        return [
            jnp.where(dim_ids == values[3 * k + 2 : 3 * k + 3], 1.0, 0.0)
            for k in range(3)
        ]

    def choose(half):
        values = table[half]
        hots = hot_rows(half)
        free = 1.0 - (hots[0] + hots[1] + hots[2])
        nothing = jnp.zeros((3 * dims, 128), F32)
        pad = jnp.zeros((13, 128), F32)
        blocks = []
        for k in range(3):
            minus = -hots[k]
            for side in range(2):
                edge = values[3 * k + side : 3 * k + side + 1]
                high = edge.astype(BF16).astype(F32)
                middle = (edge - high).astype(BF16).astype(F32)
                low = edge - high - middle
                blocks.append([minus, minus, minus, nothing, high, middle, low, pad])
        offset = jnp.full((1, 128), -3.0, F32)
        none = jnp.zeros((15, 128), F32)
        blocks.append([nothing, free, free, free, offset, none])
        for n, block in enumerate(blocks):
            block = jnp.concatenate(block, axis=0).T.astype(BF16)
            for group in range(128 // GROUP):
                chosen[half, group, n * GROUP : n * GROUP + GROUP, :] = block[
                    group * GROUP : group * GROUP + GROUP
                ]

    choose(z_hi)

    pl.semaphore_wait(barrier, len(peers))
    table_copy = send(table.at[z_hi], table_sems.at[0], table_sems.at[1], partner)
    for i, j in plane_steps:
        send(pieces.at[plane], piece_sends.at[0], piece_recvs.at[i], at_p(i, j))
    for i in hubs:
        pl.semaphore_signal(ready, inc=1, device_id=at_z(i), device_id_type=MESH)

    row = lax.broadcasted_iota(jnp.int32, (16, width), 0)
    ones = jnp.where(row < 3, 1.0, 0.0).astype(BF16)

    def points_of(chunk):
        first = ((y + n_y - chunk) % n_y) * n_a
        tiles = [pieces[first + i] for i in range(n_a)]
        points = jnp.concatenate(
            [
                jnp.concatenate(
                    [t[:, local * i : local * i + local] for t in tiles], axis=1
                )
                for i in range(dims // 8)
            ],
            axis=0,
        )
        return points * inverse

    def prepare(chunk):
        point = points_of(chunk)
        erf_high = erf_of(float(GRID) * inverse - point)
        mass = 0.5 * (erf_high + erf_of(point))
        logs = jnp.log(mass) * LOG2E
        rights[:, chunk * width : chunk * width + width] = jnp.concatenate(
            list(split3(point)) + list(split3(logs)) + [ones], axis=0
        )

    def slope_of(chunk):
        point = points_of(chunk)
        beyond = float(GRID) * inverse - point
        return -(moment_of(point) + moment_of(beyond)) / (erf_of(beyond) + erf_of(point))

    def arguments(half, group, chunk, rows):
        terms = dot(
            chosen[half, group, : rows * GROUP],
            rights[:, chunk * width : chunk * width + width],
            1,
            0,
        )
        return [terms[n * GROUP : n * GROUP + GROUP] for n in range(rows)]

    def fold(part):
        total = part[:, :128]
        for j in range(1, width // 128):
            total = total + part[:, 128 * j : 128 * j + 128]
        return total

    def masses_of(half):
        groups = range(128 // GROUP)
        totals = [None for _ in groups]
        for chunk in range(n_y):
            for group in groups:
                here = slice(group * GROUP, group * GROUP + GROUP)
                terms = arguments(half, group, chunk, 7)
                first, second, third = (
                    erf_of(terms[2 * k]) - erf_of(terms[2 * k + 1]) for k in range(3)
                )
                rest = jnp.exp2(terms[6])
                rest0 = rest * first
                rest01 = rest0 * second
                within = rest01 * third
                inside[chunk, half, here, :] = within
                leaves[0, chunk, half, here, :] = rest * (second * third)
                leaves[1, chunk, half, here, :] = rest0 * third
                leaves[2, chunk, half, here, :] = rest01
                part = fold(within)
                totals[group] = part if chunk == 0 else totals[group] + part
        for group in groups:
            sums[0, half, group * GROUP : group * GROUP + GROUP, :] = totals[group]

    def moments_of(half):
        for group in range(128 // GROUP):
            here = slice(group * GROUP, group * GROUP + GROUP)
            totals = [None] * 3
            for chunk in range(n_y):
                terms = arguments(half, group, chunk, 6)
                for k in range(3):
                    moment = moment_of(terms[2 * k + 1]) - moment_of(terms[2 * k])
                    part = fold(leaves[k, chunk, half, here, :] * moment)
                    totals[k] = part if totals[k] is None else totals[k] + part
            for k in range(3):
                sums[k + 1, half, here, :] = totals[k]

    for i in range(n_y):
        count = n_a - 1 if i == 0 else n_a
        wait_bytes(pieces.at[0:count], piece_recvs.at[i])
        prepare(i)

    def half_block(step, carry):
        @pl.when(step == 1)
        def _():
            table_copy.wait_recv()
            choose(1 - z_hi)

        masses_of(jnp.where(step == 0, z_hi, 1 - z_hi))
        return carry

    lax.fori_loop(0, n_hi, half_block, 0)

    totals = row_sums(jnp.concatenate([sums[0, half] for half in range(n_hi)], axis=0))
    for half in range(n_hi):
        est[z, half : half + 1] = totals[:, 128 * half : 128 * half + 128]
    if hubs:
        pl.semaphore_wait(ready, len(hubs))
    for i in z_steps:
        send(est.at[z], est_sems.at[0], est_sems.at[1], at_z(i))
    def half_moments(half, carry):
        moments_of(half)
        return carry

    lax.fori_loop(0, n_hi, half_moments, 0)
    derivs = []
    slopes = [split3(slope_of(chunk)) for chunk in range(n_y)]
    for half in range(n_hi):
        hots = hot_rows(half)
        free = 1.0 - (hots[0] + hots[1] + hots[2])
        total = jnp.zeros((dims, 128), F32)
        for chunk in range(n_y):
            steep, steep_rest, _ = slopes[chunk]
            within, within_rest, _ = split3(inside[chunk, half])
            total = total + dot(steep, within, 1, 1)
            total = total + dot(steep_rest, within, 1, 1)
            total = total + dot(steep, within_rest, 1, 1)
        total = total * free
        for k in range(3):
            total = total + hots[k] * row_sums(sums[k + 1, half])
        derivs.append(total)
    smoothing = 1.0 / TABLE_ROWS
    counts = jnp.concatenate([table[half][9:10] for half in range(n_hi)], axis=0)
    target = jnp.log(counts / TABLE_ROWS + smoothing)
    wait_bytes(est.at[0 : n_z - 1], est_sems.at[1])
    estimate = est[0]
    for i in range(1, n_z):
        estimate = estimate + est[i]
    estimate = estimate / sample_total
    log_est = jnp.log(estimate + smoothing)
    weight = 2.0 * (log_est - target) / (query_total * (estimate + smoothing))
    weighted = derivs[0] * weight[0:1]
    for half in range(1, n_hi):
        weighted = weighted + derivs[half] * weight[half : half + 1]
    weighted = jnp.concatenate([weighted, jnp.zeros((128 - dims, 128), F32)], axis=0)
    share = row_sums(weighted) * (SLOPE_SCALE / sample_total)

    grad_p[plane] = share
    for i, j in plane_steps:
        send(grad_p.at[plane], gp_sems.at[0], gp_sems.at[1], at_p(i, j))
    log_ref[...] = jnp.where(z_hi == 0, log_est[0:1], log_est[1:2])
    flat = n_p - 1
    wait_bytes(grad_p.at[0:flat], gp_sems.at[1])
    share = grad_p[0]
    for i in range(1, n_p):
        share = share + grad_p[i]
    grad_z[z] = share
    for i in z_steps:
        send(grad_z.at[z], gz_sems.at[0], gz_sems.at[1], at_z(i))
    table_copy.wait_send()
    wait_bytes(pieces.at[0:flat], piece_sends.at[0])
    wait_bytes(est.at[0 : n_z - 1], est_sems.at[0])
    wait_bytes(grad_p.at[0:flat], gp_sems.at[0])
    wait_bytes(grad_z.at[0 : n_z - 1], gz_sems.at[1])
    share = grad_z[0]
    for i in range(1, n_z):
        share = share + grad_z[i]
    grad_ref[...] = share[:, :dims]
    wait_bytes(grad_z.at[0 : n_z - 1], gz_sems.at[0])


def on_device(sizes, samples, bounds, spread, counts):
    n_hi, n_y, n_a, n_lo = sizes
    n_z = n_hi * n_lo
    dims, local = samples.shape
    width = local * n_a
    queries = bounds.shape[2]
    sample_total = local * n_hi * n_y * n_a * n_lo
    query_total = queries * n_hi * n_y * n_a
    vmem = pl.BlockSpec(memory_space=pltpu.VMEM)
    whole = pl.BlockSpec(memory_space=pltpu.HBM)
    dma = pltpu.SemaphoreType.DMA
    inputs = [
        pltpu.with_memory_space_constraint(value, pltpu.HBM)
        for value in (
            samples,
            bounds,
            spread.reshape(1, dims),
            counts.reshape(1, queries),
        )
    ]
    log_est, grad = pl.pallas_call(
        functools.partial(kernel, sizes, float(sample_total), float(query_total)),
        out_shape=(
            jax.ShapeDtypeStruct((1, queries), F32),
            jax.ShapeDtypeStruct((1, dims), F32),
        ),
        in_specs=[whole] * 4,
        out_specs=(vmem, vmem),
        scratch_shapes=[
            pltpu.VMEM((dims, local), F32),
            pltpu.VMEM((2, dims, queries), jnp.int32),
            pltpu.VMEM((1, dims), F32),
            pltpu.VMEM((1, queries), jnp.int32),
            pltpu.VMEM((n_hi, 16, 128), F32),
            pltpu.VMEM((n_y * n_a, 8, 128), F32),
            pltpu.VMEM((DEPTH, n_y * width), BF16),
            pltpu.VMEM((n_hi, 128 // GROUP, 7 * GROUP, DEPTH), BF16),
            pltpu.VMEM((n_y, n_hi, 128, width), F32),
            pltpu.VMEM((3, n_y, n_hi, 128, width), F32),
            pltpu.VMEM((4, n_hi, 128, 128), F32),
            pltpu.VMEM((n_z, n_hi, 128), F32),
            pltpu.VMEM((n_z, 1, 128), F32),
            pltpu.VMEM((n_y * n_a, 1, 128), F32),
            dma((4,)),
            dma((2,)),
            dma((1,)),
            dma((n_y,)),
            dma((2,)),
            dma((2,)),
            dma((2,)),
            pltpu.SemaphoreType.REGULAR,
        ],
        compiler_params=pltpu.CompilerParams(
            collective_id=0, has_side_effects=True, vmem_limit_bytes=40 * 1024 * 1024
        ),
    )(*inputs)
    return log_est.reshape(queries), grad.reshape(dims)


def solution(mesh):
    n_blk = mesh.shape["blk"]
    sizes = (2, 4, n_blk // 8, mesh.shape["grp"])
    return jax.shard_map(
        functools.partial(on_device, sizes),
        mesh=mesh,
        in_specs=(P(None, ("blk", "grp")), P(None, None, "blk"), P(), P("blk")),
        out_specs=(P("blk"), P()),
        check_vma=False,
    )
```

```python
import functools
import math

import jax
import jax.numpy as jnp
from jax import lax
from jax.experimental import pallas as pl
from jax.experimental.pallas import tpu as pltpu
from jax.sharding import PartitionSpec as P

TABLE_ROWS = 1048576
MESH = pl.DeviceIdType.MESH
F32 = jnp.float32
BF16 = jnp.bfloat16

UNIT = math.sqrt(math.log2(math.e) / 2.0)
LOG2E = math.log2(math.e)
ERF_COEFS = (
    0.939437726891315,
    0.059304200409920856,
    -7.37546114627212e-05,
    -0.00017348738576916883,
    1.7241095109019066e-05,
    -7.97342195757559e-07,
    1.4676678471795133e-08,
)
SLOPE_SCALE = 2.0 / (math.sqrt(2.0 * math.pi) * UNIT)

GRID = 256
GROUP = 128
REACH = 4
DEPTH = 208


def erf_of(v):
    w = v * v
    poly = ERF_COEFS[-1] * w + ERF_COEFS[-2]
    for coef in ERF_COEFS[-3::-1]:
        poly = poly * w + coef
    return jnp.tanh(v * poly)


def moment_of(v):
    return v * jnp.exp2(-(v * v))


def split3(x):
    high = x.astype(BF16)
    rest = x - high.astype(F32)
    middle = rest.astype(BF16)
    low = (rest - middle.astype(F32)).astype(BF16)
    return high, middle, low


def dot(a, b, a_dim, b_dim):
    return lax.dot_general(
        a, b, (((a_dim,), (b_dim,)), ((), ())), preferred_element_type=F32
    )


def row_sums(x):
    pieces = jnp.concatenate(split3(x), axis=1)
    return dot(jnp.ones((8, pieces.shape[1]), BF16), pieces, 1, 1)[:1]


def kernel(
    sizes,
    sample_total,
    query_total,
    samples_hbm,
    bounds_hbm,
    spread_hbm,
    counts_hbm,
    log_ref,
    grad_ref,
    samples_ref,
    bounds_ref,
    spread_ref,
    counts_ref,
    table,
    pieces,
    rights,
    chosen,
    inside,
    leaves,
    sums,
    est,
    grad_z,
    grad_p,
    input_sems,
    table_sems,
    piece_sends,
    piece_recvs,
    est_sems,
    gz_sems,
    gp_sems,
    ready,
):
    n_hi, n_y, n_a, n_lo = sizes
    n_z = n_hi * n_lo
    n_p = n_y * n_a
    dims, local = samples_ref.shape
    width = local * n_a

    inputs = []
    for i, (src, dst) in enumerate(
        (
            (samples_hbm, samples_ref),
            (spread_hbm, spread_ref),
            (bounds_hbm, bounds_ref),
            (counts_hbm, counts_ref),
        )
    ):
        copy = pltpu.make_async_copy(src, dst, input_sems.at[i])
        copy.start()
        inputs.append(copy)

    blk = lax.axis_index("blk")
    z_lo = lax.axis_index("grp")
    z_hi = blk // n_p
    plane = blk % n_p
    y = plane // n_a
    a = plane % n_a
    z = z_hi * n_lo + z_lo

    def at_z(step):
        other = (z + step) % n_z
        return ((other // n_lo) * n_p + plane, other % n_lo)

    def at_p(y_step, a_step):
        return (z_hi * n_p + ((y + y_step) % n_y) * n_a + (a + a_step) % n_a, z_lo)

    partner = ((1 - z_hi) * n_p + plane, (z_lo + n_lo // 2) % n_lo)
    plane_steps = sorted(
        ((i, j) for i in range(n_y) for j in range(n_a) if i or j),
        key=lambda s: -2 * min(s[0], n_y - s[0]) - min(s[1], n_a - s[1]),
    )
    z_steps = sorted(range(1, n_z), key=lambda i: -min(i, n_z - i))

    barrier = pltpu.get_barrier_semaphore()
    peers = []
    near = [i for i in z_steps if min(i, n_z - i) <= REACH]
    hubs = [i for i in near if min(i, n_z - i) == REACH]
    peers += [at_z(i) for i in near]
    peers += [at_p(i, j) for i, j in plane_steps]
    for peer in peers:
        pl.semaphore_signal(barrier, inc=1, device_id=peer, device_id_type=MESH)

    def send(ref, send_sem, recv_sem, peer):
        copy = pltpu.make_async_remote_copy(
            src_ref=ref,
            dst_ref=ref,
            send_sem=send_sem,
            recv_sem=recv_sem,
            device_id=peer,
            device_id_type=MESH,
        )
        copy.start()
        return copy

    def wait_bytes(ref, sem):
        pltpu.make_async_copy(ref, ref, sem).wait()

    inputs[0].wait()
    x = samples_ref[...]
    pieces[plane] = jnp.concatenate(
        [x[8 * i : 8 * i + 8] for i in range(dims // 8)], axis=1
    )
    inputs[1].wait()
    inverse = UNIT / spread_ref[...]
    eye = lax.broadcasted_iota(jnp.int32, (dims, dims), 0) == lax.broadcasted_iota(
        jnp.int32, (dims, dims), 1
    )
    inverse = jnp.sum(jnp.where(eye, inverse, 0.0), axis=1, keepdims=True)
    inputs[2].wait()
    inputs[3].wait()
    lower = bounds_ref[0]
    upper = bounds_ref[1]
    restricted = (upper - lower) < GRID
    below = lax.broadcasted_iota(jnp.int32, (dims, dims), 0) > lax.broadcasted_iota(
        jnp.int32, (dims, dims), 1
    )
    rank = dot(
        jnp.where(below, 1.0, 0.0).astype(BF16),
        jnp.where(restricted, 1.0, 0.0).astype(BF16),
        1,
        0,
    )
    dim_ids = lax.broadcasted_iota(jnp.int32, (dims, 128), 0).astype(F32)
    scaled_upper = upper.astype(F32) * inverse
    scaled_lower = lower.astype(F32) * inverse
    rows = []
    for k in range(3):
        mine = restricted & (rank == float(k))
        for values in (scaled_upper, scaled_lower, dim_ids):
            rows.append(
                jnp.sum(jnp.where(mine, values, 0.0), axis=0, keepdims=True)
            )
    rows.append(counts_ref[...].astype(F32))
    rows.append(jnp.zeros((6, 128), F32))
    table[z_hi] = jnp.concatenate(rows, axis=0)
    def hot_rows(half):
        values = table[half]
        return [
            jnp.where(dim_ids == values[3 * k + 2 : 3 * k + 3], 1.0, 0.0)
            for k in range(3)
        ]

    def choose(half):
        values = table[half]
        hots = hot_rows(half)
        free = 1.0 - (hots[0] + hots[1] + hots[2])
        nothing = jnp.zeros((3 * dims, 128), F32)
        pad = jnp.zeros((13, 128), F32)
        blocks = []
        for k in range(3):
            minus = -hots[k]
            for side in range(2):
                edge = values[3 * k + side : 3 * k + side + 1]
                high = edge.astype(BF16).astype(F32)
                middle = (edge - high).astype(BF16).astype(F32)
                low = edge - high - middle
                blocks.append([minus, minus, minus, nothing, high, middle, low, pad])
        offset = jnp.full((1, 128), -3.0, F32)
        none = jnp.zeros((15, 128), F32)
        blocks.append([nothing, free, free, free, offset, none])
        for n, block in enumerate(blocks):
            block = jnp.concatenate(block, axis=0).T.astype(BF16)
            for group in range(128 // GROUP):
                chosen[half, group, n * GROUP : n * GROUP + GROUP, :] = block[
                    group * GROUP : group * GROUP + GROUP
                ]

    choose(z_hi)

    pl.semaphore_wait(barrier, len(peers))
    table_copy = send(table.at[z_hi], table_sems.at[0], table_sems.at[1], partner)
    for i, j in plane_steps:
        send(pieces.at[plane], piece_sends.at[0], piece_recvs.at[i], at_p(i, j))
    for i in hubs:
        pl.semaphore_signal(ready, inc=1, device_id=at_z(i), device_id_type=MESH)

    row = lax.broadcasted_iota(jnp.int32, (16, width), 0)
    ones = jnp.where(row < 3, 1.0, 0.0).astype(BF16)

    def points_of(chunk):
        first = ((y + n_y - chunk) % n_y) * n_a
        tiles = [pieces[first + i] for i in range(n_a)]
        points = jnp.concatenate(
            [
                jnp.concatenate(
                    [t[:, local * i : local * i + local] for t in tiles], axis=1
                )
                for i in range(dims // 8)
            ],
            axis=0,
        )
        return points * inverse

    def prepare(chunk):
        point = points_of(chunk)
        erf_high = erf_of(float(GRID) * inverse - point)
        mass = 0.5 * (erf_high + erf_of(point))
        logs = jnp.log(mass) * LOG2E
        rights[:, chunk * width : chunk * width + width] = jnp.concatenate(
            list(split3(point)) + list(split3(logs)) + [ones], axis=0
        )

    def slope_of(chunk):
        point = points_of(chunk)
        beyond = float(GRID) * inverse - point
        return -(moment_of(point) + moment_of(beyond)) / (erf_of(beyond) + erf_of(point))

    def arguments(half, group, chunk, rows):
        terms = dot(
            chosen[half, group, : rows * GROUP],
            rights[:, chunk * width : chunk * width + width],
            1,
            0,
        )
        return [terms[n * GROUP : n * GROUP + GROUP] for n in range(rows)]

    def fold(part):
        total = part[:, :128]
        for j in range(1, width // 128):
            total = total + part[:, 128 * j : 128 * j + 128]
        return total

    def masses_of(half):
        groups = range(128 // GROUP)
        totals = [None for _ in groups]
        for chunk in range(n_y):
            for group in groups:
                here = slice(group * GROUP, group * GROUP + GROUP)
                terms = arguments(half, group, chunk, 7)
                first, second, third = (
                    erf_of(terms[2 * k]) - erf_of(terms[2 * k + 1]) for k in range(3)
                )
                rest = jnp.exp2(terms[6])
                rest0 = rest * first
                rest01 = rest0 * second
                within = rest01 * third
                inside[chunk, half, here, :] = within
                leaves[0, chunk, half, here, :] = rest * (second * third)
                leaves[1, chunk, half, here, :] = rest0 * third
                leaves[2, chunk, half, here, :] = rest01
                part = fold(within)
                totals[group] = part if chunk == 0 else totals[group] + part
        for group in groups:
            sums[0, half, group * GROUP : group * GROUP + GROUP, :] = totals[group]

    def moments_of(half):
        for group in range(128 // GROUP):
            here = slice(group * GROUP, group * GROUP + GROUP)
            totals = [None] * 3
            for chunk in range(n_y):
                terms = arguments(half, group, chunk, 6)
                for k in range(3):
                    moment = moment_of(terms[2 * k + 1]) - moment_of(terms[2 * k])
                    part = fold(leaves[k, chunk, half, here, :] * moment)
                    totals[k] = part if totals[k] is None else totals[k] + part
            for k in range(3):
                sums[k + 1, half, here, :] = totals[k]

    for i in range(n_y):
        count = n_a - 1 if i == 0 else n_a
        wait_bytes(pieces.at[0:count], piece_recvs.at[i])
        prepare(i)

    def half_block(step, carry):
        @pl.when(step == 1)
        def _():
            table_copy.wait_recv()
            choose(1 - z_hi)

        masses_of(jnp.where(step == 0, z_hi, 1 - z_hi))
        return carry

    lax.fori_loop(0, n_hi, half_block, 0)

    totals = row_sums(jnp.concatenate([sums[0, half] for half in range(n_hi)], axis=0))
    for half in range(n_hi):
        est[z, half : half + 1] = totals[:, 128 * half : 128 * half + 128]
    if hubs:
        pl.semaphore_wait(ready, len(hubs))
    for i in z_steps:
        send(est.at[z], est_sems.at[0], est_sems.at[1], at_z(i))
    def half_moments(half, carry):
        moments_of(half)
        return carry

    lax.fori_loop(0, n_hi, half_moments, 0)
    derivs = []
    slopes = [split3(slope_of(chunk)) for chunk in range(n_y)]
    for half in range(n_hi):
        hots = hot_rows(half)
        free = 1.0 - (hots[0] + hots[1] + hots[2])
        total = jnp.zeros((dims, 128), F32)
        for chunk in range(n_y):
            steep, steep_rest, _ = slopes[chunk]
            within, within_rest, _ = split3(inside[chunk, half])
            total = total + dot(steep, within, 1, 1)
            total = total + dot(steep_rest, within, 1, 1)
            total = total + dot(steep, within_rest, 1, 1)
        total = total * free
        for k in range(3):
            total = total + hots[k] * row_sums(sums[k + 1, half])
        derivs.append(total)
    smoothing = 1.0 / TABLE_ROWS
    counts = jnp.concatenate([table[half][9:10] for half in range(n_hi)], axis=0)
    target = jnp.log(counts / TABLE_ROWS + smoothing)
    wait_bytes(est.at[0 : n_z - 1], est_sems.at[1])
    estimate = est[0]
    for i in range(1, n_z):
        estimate = estimate + est[i]
    estimate = estimate / sample_total
    log_est = jnp.log(estimate + smoothing)
    weight = 2.0 * (log_est - target) / (query_total * (estimate + smoothing))
    weighted = derivs[0] * weight[0:1]
    for half in range(1, n_hi):
        weighted = weighted + derivs[half] * weight[half : half + 1]
    weighted = jnp.concatenate([weighted, jnp.zeros((128 - dims, 128), F32)], axis=0)
    share = row_sums(weighted) * (SLOPE_SCALE / sample_total)

    grad_p[plane] = share
    for i, j in plane_steps:
        send(grad_p.at[plane], gp_sems.at[0], gp_sems.at[1], at_p(i, j))
    log_ref[...] = jnp.where(z_hi == 0, log_est[0:1], log_est[1:2])
    flat = n_p - 1
    wait_bytes(grad_p.at[0:flat], gp_sems.at[1])
    share = grad_p[0]
    for i in range(1, n_p):
        share = share + grad_p[i]
    grad_z[z] = share
    for i in z_steps:
        send(grad_z.at[z], gz_sems.at[0], gz_sems.at[1], at_z(i))
    table_copy.wait_send()
    wait_bytes(pieces.at[0:flat], piece_sends.at[0])
    wait_bytes(est.at[0 : n_z - 1], est_sems.at[0])
    wait_bytes(grad_p.at[0:flat], gp_sems.at[0])
    wait_bytes(grad_z.at[0 : n_z - 1], gz_sems.at[1])
    share = grad_z[0]
    for i in range(1, n_z):
        share = share + grad_z[i]
    grad_ref[...] = share[:, :dims]
    wait_bytes(grad_z.at[0 : n_z - 1], gz_sems.at[0])


def on_device(sizes, samples, bounds, spread, counts):
    n_hi, n_y, n_a, n_lo = sizes
    n_z = n_hi * n_lo
    dims, local = samples.shape
    width = local * n_a
    queries = bounds.shape[2]
    sample_total = local * n_hi * n_y * n_a * n_lo
    query_total = queries * n_hi * n_y * n_a
    vmem = pl.BlockSpec(memory_space=pltpu.VMEM)
    whole = pl.BlockSpec(memory_space=pltpu.HBM)
    dma = pltpu.SemaphoreType.DMA
    inputs = [
        pltpu.with_memory_space_constraint(value, pltpu.HBM)
        for value in (
            samples,
            bounds,
            spread.reshape(1, dims),
            counts.reshape(1, queries),
        )
    ]
    log_est, grad = pl.pallas_call(
        functools.partial(kernel, sizes, float(sample_total), float(query_total)),
        out_shape=(
            jax.ShapeDtypeStruct((1, queries), F32),
            jax.ShapeDtypeStruct((1, dims), F32),
        ),
        in_specs=[whole] * 4,
        out_specs=(vmem, vmem),
        scratch_shapes=[
            pltpu.VMEM((dims, local), F32),
            pltpu.VMEM((2, dims, queries), jnp.int32),
            pltpu.VMEM((1, dims), F32),
            pltpu.VMEM((1, queries), jnp.int32),
            pltpu.VMEM((n_hi, 16, 128), F32),
            pltpu.VMEM((n_y * n_a, 8, 128), F32),
            pltpu.VMEM((DEPTH, n_y * width), BF16),
            pltpu.VMEM((n_hi, 128 // GROUP, 7 * GROUP, DEPTH), BF16),
            pltpu.VMEM((n_y, n_hi, 128, width), F32),
            pltpu.VMEM((3, n_y, n_hi, 128, width), F32),
            pltpu.VMEM((4, n_hi, 128, 128), F32),
            pltpu.VMEM((n_z, n_hi, 128), F32),
            pltpu.VMEM((n_z, 1, 128), F32),
            pltpu.VMEM((n_y * n_a, 1, 128), F32),
            dma((4,)),
            dma((2,)),
            dma((1,)),
            dma((n_y,)),
            dma((2,)),
            dma((2,)),
            dma((2,)),
            pltpu.SemaphoreType.REGULAR,
        ],
        compiler_params=pltpu.CompilerParams(
            collective_id=0, has_side_effects=True, vmem_limit_bytes=40 * 1024 * 1024
        ),
    )(*inputs)
    return log_est.reshape(queries), grad.reshape(dims)


def solution(mesh):
    n_blk = mesh.shape["blk"]
    sizes = (2, 4, n_blk // 8, mesh.shape["grp"])
    return jax.shard_map(
        functools.partial(on_device, sizes),
        mesh=mesh,
        in_specs=(P(None, ("blk", "grp")), P(None, None, "blk"), P(), P("blk")),
        out_specs=(P("blk"), P()),
        check_vma=False,
    )
```
